32 devices in a mesh: groups: 2 (over x), chan: 16 (over z, y, core).
Axes of the slice: x: 2, y: 2, z: 4, core: 2. Of those that a mesh axis runs over, the one named last changes fastest.
Arguments:
- psi_prev: float32 [1024, 32, 128], P(('groups', 'chan')), parts along dimension 0, may hold values from -6 to 6
- psi_cur: float32 [1024, 32, 128], P(('groups', 'chan')), parts along dimension 0, may hold values from -6 to 6
- kin_stretch: float32 [32, 32], replicated, may hold values from -0.75 to 0.75
- kin_radius: float32 [128, 128], replicated, may hold values from -0.375 to 0.375
- potential: float32 [3, 32, 128], replicated, may hold values from -4 to 4
- angular: float32 [6, 512, 512], P('groups'), parts along dimension 0, may hold values from -0.4375 to 0.4375
- pattern: int32 [16, 8], P('groups'), parts along dimension 0, may hold values 0 or 1
- quanta: int32 [1024, 2], P(('groups', 'chan')), parts along dimension 0, may hold values from 0 to 39
Outputs:
- prev_out: float32 [1024, 32, 128], P(('groups', 'chan')), parts along dimension 0
- cur_out: float32 [1024, 32, 128], P(('groups', 'chan')), parts along dimension 0
- norms: float32 [6], P('groups'), parts along dimension 0
The draws below stay inside these ranges and needn't reach their ends.
There are 2 independent parts, one for each index of `groups`. The reference program is written for one: setup_inputs(seed, part) draws one part's arguments, and reference() takes and returns one part's arrays. A program takes and returns all parts, laid end to end along the dimension named above; an argument that names none is the same for every part. Nothing has to cross between parts.
All inputs are finite; a program needn't handle non-finite values.
Results may differ from the reference program's by a relative error of at most 0.00085.
Values sent between devices are 32-bit elements; how exact they have to be, the bound alone decides.
No kernel may reach another device: no remote copies, remote signals or barrier semaphores. Data moves between devices by JAX's collectives and lax.ppermute only.
A program may use at most 64 MiB of HBM per device.

```python
import jax
import jax.numpy as jnp
from jax import lax

C = 512
NR = 32
NSR = 128
LAM = 3
CB = 64
JL_MAX = 40
ITERS = 3
NBLK = 8


def place_ends(result, stream_key, least, largest):
    shape = result.shape
    spot = [jax.random.randint(jax.random.fold_in(stream_key, axis), (), 0, shape[axis]) for axis in range(len(shape))]
    result = result.at[tuple(spot)].set(least)
    longest = shape.index(max(shape))
    spot[longest] = (spot[longest] + 1) % shape[longest]
    return result.at[tuple(spot)].set(largest)


def shard_levels(key, dims, shards, smallest, high):
    loudness = 1.0
    for axis_at, blocks in shards:
        draws = jax.random.uniform(jax.random.fold_in(jax.random.fold_in(key, 6), axis_at), (blocks,), jnp.float32, smallest / len(shards), high / len(shards))
        loudness = loudness * jnp.repeat(jnp.exp(draws), dims[axis_at] // blocks).reshape((-1,) + (1,) * (len(dims) - 1 - axis_at))
    return loudness


def scatter_about(stream_key, shape, spread, limit, cuts=(), kind=jnp.bfloat16):
    factor_of = shard_levels(stream_key, shape, cuts, -0.22, 0.18) if cuts else 1.0
    result = jax.random.normal(stream_key, shape, jnp.float32) * spread * factor_of
    return jnp.minimum(jnp.maximum(result, -limit), limit).astype(kind)


def setup_inputs(seed: int = 0, part: int = 0) -> dict:
    key_list = jax.random.split(jax.random.key(seed), 9)
    part_splits = jax.random.split(jax.random.fold_in(key_list[8], part), 9)
    return {
        "psi_prev": scatter_about(part_splits[0], (C, NR, NSR), 1.0, 6.0, ((0, 16),), jnp.float32),
        "psi_cur": scatter_about(part_splits[1], (C, NR, NSR), 1.0, 6.0, ((0, 16),), jnp.float32),
        "kin_stretch": scatter_about(key_list[2], (NR, NR), (0.3 / NR ** 0.5), 0.75, (), jnp.float32),
        "kin_radius": scatter_about(key_list[3], (NSR, NSR), (0.3 / NSR ** 0.5), 0.375, (), jnp.float32),
        "potential": scatter_about(key_list[4], (LAM, NR, NSR), 0.5, 4.0, (), jnp.float32),
        "angular": scatter_about(part_splits[5], (LAM, C, C), (0.7 / C ** 0.5), 0.4375, (), jnp.float32),
        "pattern": place_ends((jax.random.randint(part_splits[6], (NBLK, NBLK), 0, 2) < 1).astype(jnp.int32), jax.random.fold_in(part_splits[6], 1), 0, 1),
        "quanta": place_ends(jax.random.randint(part_splits[7], (C, 2), 0, JL_MAX), jax.random.fold_in(part_splits[7], 1), 0, JL_MAX - 1).astype(jnp.int32),
    }


def barrier_of(quanta, nr, nsr):
    jval = quanta[:, 0].astype(jnp.float32)
    lval = quanta[:, 1].astype(jnp.float32)
    scale = 0.15 / (JL_MAX * (JL_MAX - 1))
    stretch = 1.0 + jnp.arange(nr, dtype=jnp.float32) / nr
    radius = 1.0 + 3.0 * jnp.arange(nsr, dtype=jnp.float32) / nsr
    orbital = scale * (lval * (lval + 1.0))[:, None, None] / (radius * radius)[None, None, :]
    rotation = scale * (jval * (jval + 1.0))[:, None, None] / (stretch * stretch)[None, :, None]
    return orbital + rotation - 0.1


def reference(psi_prev, psi_cur, kin_stretch, kin_radius, potential, angular, pattern, quanta):
    hp = lax.Precision.HIGHEST
    expanded = jnp.repeat(jnp.repeat(pattern.astype(jnp.float32), CB, 0), CB, 1)
    coupling = angular * expanded[None]
    barrier = barrier_of(quanta, NR, NSR)
    flat_pot = potential.reshape(LAM, NR * NSR)

    def apply_h(field):
        out = jnp.einsum("ae,ceb->cab", kin_stretch, field, precision=hp)
        out = out + jnp.einsum("cae,eb->cab", field, kin_radius, precision=hp)
        out = out + barrier * field
        flat = field.reshape(C, NR * NSR)
        mixed = jnp.einsum("lcd,ldp->cp", coupling, flat_pot[:, None, :] * flat[None], precision=hp)
        return out + mixed.reshape(C, NR, NSR)

    prev, cur = psi_prev, psi_cur
    norm_list = []
    for step in range(ITERS):
        nxt = 2.0 * apply_h(cur) - prev
        norm_list.append(jnp.sum(nxt * nxt) / (C * NR * NSR))
        prev, cur = cur, nxt
    return prev, cur, jnp.stack(norm_list).astype(jnp.float32)
```

```python
import functools

import jax
import jax.numpy as jnp
import numpy as np
from jax import lax
from jax.experimental import pallas as pl
from jax.experimental.pallas import tpu as pltpu
from jax.sharding import PartitionSpec as P

JL_MAX = 40
ITERS = 3
F32 = jnp.float32
BF16 = jnp.bfloat16
HP = lax.Precision.HIGHEST
VM = pl.BlockSpec(memory_space=pltpu.VMEM)
SM = pl.BlockSpec(memory_space=pltpu.SMEM)


def natural(ref, na):
    nr = ref.shape[1]
    half = nr // na

    def load(c, al):
        return ref[c, pl.ds(al, half, stride=na), :] if na > 1 else ref[c]

    return load


def amajor(refs, na, nc, pitch=None):
    nk = na // len(refs)
    pitch = pitch or nk * nc

    def load(c, al):
        ref = refs[al // nk]
        return ref[pl.ds((al % nk) * nc + c, ref.shape[0] // pitch, stride=pitch), :]

    return load


def to_amajor_kernel(na, nc, x_ref, o_ref):
    half = o_ref.shape[0] // (na * nc)
    load = natural(x_ref, na)
    for c in range(nc):
        for al in range(na):
            o_ref[pl.ds(al * nc + c, half, stride=na * nc), :] = load(c, al)


def to_natural_kernel(na, nc, pitch, x_ref, o_ref):
    half = o_ref.shape[1] // na
    load = amajor([x_ref], na, nc, pitch)
    for c in range(nc):
        for al in range(na):
            if na > 1:
                o_ref[c, pl.ds(al, half, stride=na), :] = load(c, al)
            else:
                o_ref[c] = load(c, al)


def kinetic_kernel(na, nc, n_cur, n_prev, want_natural, *refs):
    quanta, ks, kr, rot, orb = refs[:5]
    cur_refs = refs[5 : 5 + max(n_cur, 1)]
    prev_refs = refs[5 + max(n_cur, 1) : 5 + max(n_cur, 1) + max(n_prev, 1)]
    outs = refs[5 + max(n_cur, 1) + max(n_prev, 1) :]
    u_ref = outs[0]
    cur = amajor(cur_refs, na, nc) if n_cur else natural(cur_refs[0], na)
    prev = amajor(prev_refs, na, nc) if n_prev else natural(prev_refs[0], na)
    half = u_ref.shape[0] // (na * nc)
    nb = u_ref.shape[1]
    nr = half * na
    kstr = ks[...]
    krad = kr[...]
    rotation = rot[...]
    orbital = orb[...]
    scale = np.float32(0.3 / (JL_MAX * (JL_MAX - 1)))
    group = min(8, nc)
    for start in range(0, nc, group):
        tiles = []
        for c in range(start, start + group):
            tiles.append(jnp.concatenate([cur(c, al) for al in range(na)], 0))
        mixed_a = jnp.dot(kstr, jnp.concatenate(tiles, 1), precision=HP, preferred_element_type=F32)
        mixed_b = jnp.dot(jnp.concatenate(tiles, 0), krad, precision=HP, preferred_element_type=F32)
        for i, x in enumerate(tiles):
            c = start + i
            j = quanta[c, 0].astype(F32)
            l = quanta[c, 1].astype(F32)
            barrier = orbital * (scale * (l * (l + 1.0))) + rotation * (scale * (j * (j + 1.0))) - 0.2
            before = jnp.concatenate([prev(c, al) for al in range(na)], 0)
            y = mixed_a[:, i * nb : (i + 1) * nb] + mixed_b[i * nr : (i + 1) * nr] + barrier * x - before
            for al in range(na):
                u_ref[pl.ds(al * nc + c, half, stride=na * nc), :] = y[al * half : (al + 1) * half]
                if want_natural:
                    piece = x[al * half : (al + 1) * half]
                    if na > 1:
                        outs[1][c, pl.ds(al, half, stride=na), :] = piece
                    else:
                        outs[1][c] = piece


def coupling_kernel(cb, side_ref, pat_ref, ang_ref, hi_ref, lo_ref):
    ch = ang_ref.shape[1]
    mine = side_ref[0]
    cols = (mine + pl.program_id(1)) % 2
    nblk = ch // cb
    lane = lax.broadcasted_iota(jnp.int32, (cb, ch), 1) // cb
    for rb in range(nblk):
        factor = jnp.zeros((cb, ch), F32)
        for k in range(nblk):
            p = pat_ref[mine * nblk + rb, cols * nblk + k].astype(F32)
            factor = jnp.where(lane == k, p, factor)
        val = ang_ref[0, rb * cb : (rb + 1) * cb, :] * factor
        hi = val.astype(BF16)
        hi_ref[rb * cb : (rb + 1) * cb, :] = hi
        lo_ref[rb * cb : (rb + 1) * cb, :] = (val - hi.astype(F32)).astype(BF16)


def mix_kernel(lam, al0, u_na, n_norm, *refs):
    hi, lo, pot, u, own, oth = refs[:6]
    norms = refs[6 : 6 + n_norm]
    out, sq = refs[6 + n_norm], (refs[7 + n_norm] if not n_norm else None)
    half, nk, nc, nb = own.shape
    ch = half * nc
    total = jnp.zeros((8, nb), F32)
    step = 2 if nk % 2 == 0 else 1
    for k0 in range(0, nk, step):
        ks = range(k0, k0 + step)
        x = jnp.concatenate(
            [jnp.concatenate([r[:, k].reshape(ch, nb) for k in ks], 1) for r in (own, oth)], 0
        )
        x_hi = x.astype(BF16)
        x_lo = (x - x_hi.astype(F32)).astype(BF16)
        acc = None
        for m in range(lam):
            rows = slice(m * ch, (m + 1) * ch)
            p = jnp.dot(hi[rows], x_hi, preferred_element_type=F32)
            p = p + jnp.dot(hi[rows], x_lo, preferred_element_type=F32)
            p = p + jnp.dot(lo[rows], x_hi, preferred_element_type=F32)
            w = jnp.concatenate([pot[m, al0 + k : al0 + k + 1] for k in ks], 1)
            acc = p * w if acc is None else acc + p * w
        for i, k in enumerate(ks):
            y = acc[:, i * nb : (i + 1) * nb].reshape(half, nc, nb)
            y = y + u[:, al0 + k]
            if n_norm:
                out[:, k * nc : (k + 1) * nc] = y
            else:
                out[:, k] = y
            total = total + jnp.sum((y * y).reshape(ch // 8, 8, nb), axis=0)
    if n_norm:
        sums = []
        per = n_norm // (ITERS - 1)
        for s in range(ITERS - 1):
            t = norms[s * per][...]
            for r in norms[s * per + 1 : (s + 1) * per]:
                t = t + r[...]
            sums.append(jnp.sum(t, axis=0, keepdims=True))
        sums.append(jnp.sum(total, axis=0, keepdims=True))
        sums.append(jnp.zeros((8 - ITERS, nb), F32))
        tile = jnp.concatenate(sums, 0)
        for s in range(half):
            out[s, nk * nc :] = tile
    else:
        sq[...] = total


def call(kernel, out_shapes, in_specs, flops=0, size=1 << 20, **kw):
    return pl.pallas_call(
        kernel,
        out_shape=out_shapes,
        in_specs=in_specs,
        out_specs=jax.tree.map(lambda _: VM, out_shapes),
        cost_estimate=pl.CostEstimate(flops=flops, bytes_accessed=size, transcendentals=0),
        **kw,
    )


def per_device(psi_prev, psi_cur, kin_stretch, kin_radius, potential, angular, pattern, quanta):
    nc, nr, nb = psi_cur.shape
    lam = potential.shape[0]
    nd = lax.axis_size("chan")
    half = nd // 2
    na = nr // half
    total_ch = nc * nd
    ch = total_ch // 2
    cb = total_ch // pattern.shape[1]
    n_chunk = 2 if na % 4 == 0 else 1
    nk = na // n_chunk
    me = lax.axis_index("chan")
    side = (me // half).astype(jnp.int32)
    groups = [[g * half + i for i in range(half)] for g in range(2)]
    across = [(i, (i + half) % nd) for i in range(nd)]
    sds = jax.ShapeDtypeStruct

    def exchange(x):
        return lax.all_to_all(x, "chan", 0, 0, tiled=True, axis_index_groups=groups)

    def swap(x):
        return lax.ppermute(x, "chan", across)

    a_of = np.arange(nr).reshape(half, na).T.reshape(-1)
    stretch = 1.0 + a_of.astype(np.float32) / np.float32(nr)
    radius = np.float32(1.0) + np.float32(3.0) * np.arange(nb, dtype=np.float32) / np.float32(nb)
    rot = jnp.asarray(np.broadcast_to((1.0 / (stretch * stretch))[:, None], (nr, nb)), F32)
    orb = jnp.asarray(np.broadcast_to((1.0 / (radius * radius))[None, :], (nr, nb)), F32)
    ks2 = 2.0 * kin_stretch.reshape(half, na, half, na).transpose(1, 0, 3, 2).reshape(nr, nr)
    kr2 = 2.0 * kin_radius
    mine = (me % half) * na
    pot2 = 2.0 * lax.dynamic_slice_in_dim(potential, mine, na, 1)

    block = pl.BlockSpec((ch, ch), lambda m, s, *_: (m, s))
    hi, lo = pl.pallas_call(
        functools.partial(coupling_kernel, cb),
        out_shape=[sds((lam * ch, 2 * ch), BF16)] * 2,
        grid_spec=pltpu.PrefetchScalarGridSpec(
            num_scalar_prefetch=2,
            grid=(lam, 2),
            in_specs=[pl.BlockSpec((1, ch, ch), lambda m, s, side, pat: (m, side[0], (side[0] + s) % 2))],
            out_specs=[block, block],
        ),
        cost_estimate=pl.CostEstimate(flops=lam * ch * ch * 8, bytes_accessed=lam * ch * ch * 16, transcendentals=0),
    )(side.reshape(1), pattern, angular)

    rows = nr * nc
    flat = sds((rows, nb), F32)

    def kinetic(cur, prev, n_cur, n_prev, want_natural):
        outs = [flat] + ([sds((nc, nr, nb), F32)] if want_natural else [])
        return call(
            functools.partial(kinetic_kernel, na, nc, n_cur, n_prev, want_natural),
            outs,
            [SM] + [VM] * (4 + len(cur) + len(prev)),
            flops=12 * rows * nb * (nr + nb),
            size=rows * nb * 12,
        )(quanta, ks2, kr2, rot, orb, *cur, *prev)

    def mix(u, own, oth, al0, norms=()):
        n = own.shape[1]
        if norms:
            outs = [sds((half, n * nc + 8, nb), F32)]
        else:
            outs = [sds((half, n, nc, nb), F32), sds((8, nb), F32)]
        return call(
            functools.partial(mix_kernel, lam, al0, na, len(norms)),
            outs,
            [VM] * (6 + len(norms)),
            flops=6 * lam * ch * 2 * ch * n * nb,
            size=ch * n * nb * 16,
        )(hi, lo, pot2, u, own, oth, *norms)

    def parts(x):
        x = x.reshape(half, na, nc, nb)
        return [x[:, i * nk : (i + 1) * nk] for i in range(n_chunk)] if n_chunk > 1 else [x]

    v1_c = call(functools.partial(to_amajor_kernel, na, nc), flat, [VM])(psi_cur)
    v1 = parts(exchange(v1_c))
    o1 = [swap(x) for x in v1]
    (u1_c,) = kinetic([psi_cur], [psi_prev], 0, 0, False)
    u1 = exchange(u1_c).reshape(half, na, nc, nb)
    v2, s2 = zip(*[mix(u1, v1[i], o1[i], i * nk) for i in range(n_chunk)])
    o2 = [swap(x) for x in v2]
    v2_c = [exchange(x).reshape(half * nk * nc, nb) for x in v2]
    (u2_c,) = kinetic(v2_c, [psi_cur], n_chunk, 0, False)
    u2 = exchange(u2_c).reshape(half, na, nc, nb)
    v3, s3 = zip(*[mix(u2, v2[i], o2[i], i * nk) for i in range(n_chunk)])
    v3 = jnp.concatenate(v3, 1)
    o3 = swap(v3)
    v3_c = exchange(v3).reshape(rows, nb)
    u3_c, prev_out = kinetic([v3_c], v2_c, 1, n_chunk, True)
    u3 = exchange(u3_c).reshape(half, na, nc, nb)
    (v4,) = mix(u3, v3, o3, 0, (*s2, *s3))
    pitch = na * nc + 8
    v4_c = exchange(v4)
    sums = jnp.sum(v4_c[:, na * nc :], axis=0)
    sums = sums + swap(sums)
    norms = jnp.sum(sums[:ITERS], axis=1) / (total_ch * nr * nb)
    cur_out = call(functools.partial(to_natural_kernel, na, nc, pitch), sds((nc, nr, nb), F32), [VM])(
        v4_c.reshape(half * pitch, nb)
    )
    return prev_out, cur_out, norms


def solution(mesh):
    return jax.shard_map(
        per_device,
        mesh=mesh,
        in_specs=(
            P(("groups", "chan"), None, None),
            P(("groups", "chan"), None, None),
            P(),
            P(),
            P(),
            P("groups", None, None),
            P("groups", None),
            P(("groups", "chan"), None),
        ),
        out_specs=(
            P(("groups", "chan"), None, None),
            P(("groups", "chan"), None, None),
            P("groups"),
        ),
        check_vma=False,
    )
```

```python
import functools

import jax
import jax.numpy as jnp
import numpy as np
from jax import lax
from jax.experimental import pallas as pl
from jax.experimental.pallas import tpu as pltpu
from jax.sharding import PartitionSpec as P

JL_MAX = 40
ITERS = 3
F32 = jnp.float32
BF16 = jnp.bfloat16
HP = lax.Precision.HIGHEST
VM = pl.BlockSpec(memory_space=pltpu.VMEM)
SM = pl.BlockSpec(memory_space=pltpu.SMEM)


def to_pieces_kernel(na, nc, spot_ref, x_ref, *outs):
    spot = spot_ref[0]
    for s, out in enumerate(outs):
        at = pl.multiple_of((spot ^ s) * na, na)
        for c in range(nc):
            out[pl.ds(c, na, stride=nc), :] = x_ref[c, pl.ds(at, na), :]


def pack_kernel(n, spot_ref, *refs):
    spot = spot_ref[0]
    pieces, outs = refs[:n], refs[n:]
    for s, piece in enumerate(pieces):
        for q, out in enumerate(outs):
            rows = out.shape[1]
            out[spot ^ s] = piece[q * rows : (q + 1) * rows]


def kinetic_kernel(na, nc, n_cur, n, *refs):
    spot_ref, quanta, ks, kr, rot, orb, prev = refs[:7]
    spot = spot_ref[0]
    if n_cur:
        pieces, u_refs, cur, y_ref = refs[7 : 7 + n_cur], refs[7 + n_cur : 7 + n_cur + n], refs[-2], refs[-1]
    else:
        pieces, u_refs, cur, y_ref = (), refs[8 : 8 + n], refs[7], refs[-1]
    nr, nb = prev.shape[1:]
    starts = [pl.multiple_of((spot ^ s) * na, na) for s in range(n)]
    kstr = ks[...]
    krad = kr[...]
    rotation = rot[...]
    orbital = orb[...]
    scale = np.float32(0.3 / (JL_MAX * (JL_MAX - 1)))
    group = min(8, nc)
    for start in range(0, nc, group):
        chans = range(start, start + group)
        for s, piece in enumerate(pieces):
            for c in chans:
                cur[c, pl.ds(starts[s], na), :] = piece[pl.ds(c, na, stride=nc), :]
        tiles = [cur[c] for c in chans]
        mixed_a = jnp.dot(kstr, jnp.concatenate(tiles, 1), precision=HP, preferred_element_type=F32)
        mixed_b = jnp.dot(jnp.concatenate(tiles, 0), krad, precision=HP, preferred_element_type=F32)
        for i, c in enumerate(chans):
            j = quanta[c, 0].astype(F32)
            l = quanta[c, 1].astype(F32)
            barrier = orbital * (scale * (l * (l + 1.0))) + rotation * (scale * (j * (j + 1.0))) - 0.2
            y = mixed_a[:, i * nb : (i + 1) * nb] + mixed_b[i * nr : (i + 1) * nr]
            y_ref[i] = y + barrier * tiles[i] - prev[c]
        for s, u in enumerate(u_refs):
            for i, c in enumerate(chans):
                u[pl.ds(c, na, stride=nc), :] = y_ref[i, pl.ds(starts[s], na), :]


def coupling_kernel(cb, side_ref, pat_ref, ang_ref, hi_ref, lo_ref):
    ch = ang_ref.shape[1]
    mine = side_ref[0]
    cols = (mine + pl.program_id(1)) % 2
    nblk = ch // cb
    lane = lax.broadcasted_iota(jnp.int32, (cb, ch), 1) // cb
    for rb in range(nblk):
        factor = jnp.zeros((cb, ch), F32)
        for k in range(nblk):
            p = pat_ref[mine * nblk + rb, cols * nblk + k].astype(F32)
            factor = jnp.where(lane == k, p, factor)
        val = ang_ref[0, rb * cb : (rb + 1) * cb, :] * factor
        hi = val.astype(BF16)
        hi_ref[rb * cb : (rb + 1) * cb, :] = hi
        lo_ref[rb * cb : (rb + 1) * cb, :] = (val - hi.astype(F32)).astype(BF16)


def mix_kernel(lam, nc, q, n, n_early, n_norm, packed, pieced, *refs):
    refs = list(refs)
    take = lambda k: [refs.pop(0) for _ in range(k)]
    spot_ref, hi, lo, pot, own, oth = take(6)
    us, early, norms = take(n), take(n_early), take(n_norm)
    out = take(1)[0] if packed else None
    sq = take(1)[0] if not n_norm else None
    pieces = take(n) if pieced else []
    tmp = out if packed else refs.pop(0)
    spot = spot_ref[0]
    half, rows, nb = own.shape
    nk, ch = rows // nc, half * nc
    for s, u in enumerate(us):
        tmp[spot ^ s] = u[q * rows : (q + 1) * rows]
    total = jnp.zeros((8, nb), F32)
    step = 2 if nk % 2 == 0 else 1
    for k0 in range(0, nk, step):
        ks = range(k0, k0 + step)
        x = jnp.concatenate(
            [jnp.concatenate([r[:, k * nc : (k + 1) * nc].reshape(ch, nb) for k in ks], 1) for r in (own, oth)], 0
        )
        x_hi = x.astype(BF16)
        x_lo = (x - x_hi.astype(F32)).astype(BF16)
        acc = None
        for m in range(lam):
            at = slice(m * ch, (m + 1) * ch)
            p = jnp.dot(hi[at], x_hi, preferred_element_type=F32)
            p = p + jnp.dot(hi[at], x_lo, preferred_element_type=F32)
            p = p + jnp.dot(lo[at], x_hi, preferred_element_type=F32)
            w = jnp.concatenate([pot[m, q * nk + k : q * nk + k + 1] for k in ks], 1)
            acc = p * w if acc is None else acc + p * w
        for i, k in enumerate(ks):
            y = acc[:, i * nb : (i + 1) * nb].reshape(half, nc, nb) + tmp[:, k * nc : (k + 1) * nc]
            tmp[:, k * nc : (k + 1) * nc] = y
            total = total + jnp.sum((y * y).reshape(ch // 8, 8, nb), axis=0)
    for s, piece in enumerate(pieces):
        for i, r in enumerate((*early, tmp)):
            piece[i * rows : (i + 1) * rows] = r[spot ^ s]
    if n_norm:
        per = n_early + 1
        for r in norms[(ITERS - 1) * per :]:
            total = total + r[...]
        sums = []
        for s in range(ITERS - 1):
            sums.append(sum((r[...] for r in norms[s * per + 1 : (s + 1) * per]), norms[s * per][...]))
        sums = [jnp.sum(t, axis=0, keepdims=True) for t in (*sums, total)]
        tile = jnp.concatenate([*sums, jnp.zeros((8 - ITERS, nb), F32)], 0)
        for piece in pieces:
            piece[(q + 1) * rows :] = tile
    else:
        sq[...] = total


def finish_kernel(na, nc, n, spot_ref, *refs):
    spot = spot_ref[0]
    pieces, out, sums, tiles = refs[:n], refs[n], refs[n + 1], refs[n + 2]
    for s, piece in enumerate(pieces):
        at = pl.multiple_of((spot ^ s) * na, na)
        for c in range(nc):
            out[c, pl.ds(at, na), :] = piece[pl.ds(c, na, stride=nc), :]
        tiles[spot ^ s] = piece[na * nc :]
    total = tiles[0]
    for s in range(1, n):
        total = total + tiles[s]
    sums[...] = total


def local(x):
    return pltpu.with_memory_space_constraint(x, pltpu.VMEM)


def call(kernel, outs, scalars, arrays, scratch=()):
    return pl.pallas_call(
        kernel,
        out_shape=outs,
        in_specs=[SM] * len(scalars) + [VM] * len(arrays),
        out_specs=[VM] * len(outs),
        scratch_shapes=list(scratch),
        cost_estimate=pl.CostEstimate(flops=0, bytes_accessed=1 << 16, transcendentals=0),
    )(*scalars, *arrays)


def per_device(psi_prev, psi_cur, kin_stretch, kin_radius, potential, angular, pattern, quanta):
    nc, nr, nb = psi_cur.shape
    lam = potential.shape[0]
    nd = lax.axis_size("chan")
    half = nd // 2
    na = nr // half
    total_ch = nc * nd
    ch = total_ch // 2
    cb = total_ch // pattern.shape[1]
    n_chunk = 2 if na % 4 == 0 else 1
    nk = na // n_chunk
    me = lax.axis_index("chan").astype(jnp.int32)
    side = (me // half).reshape(1)
    spot = (me % half).reshape(1)
    sds = jax.ShapeDtypeStruct

    def exchange(pieces):
        moved = [
            lax.ppermute(x, "chan", [(i, i ^ s) for i in range(nd)]) if s else x for s, x in enumerate(pieces)
        ]
        return [local(x) for x in moved]

    def swap(x):
        return lax.ppermute(x, "chan", [(i, (i + half) % nd) for i in range(nd)])

    stretch = np.float32(1.0) + np.arange(nr, dtype=np.float32) / np.float32(nr)
    radius = np.float32(1.0) + np.float32(3.0) * np.arange(nb, dtype=np.float32) / np.float32(nb)
    rot = jnp.asarray(np.broadcast_to((1.0 / (stretch * stretch))[:, None], (nr, nb)), F32)
    orb = jnp.asarray(np.broadcast_to((1.0 / (radius * radius))[None, :], (nr, nb)), F32)
    ks2 = 2.0 * kin_stretch
    kr2 = 2.0 * kin_radius
    pot2 = 2.0 * lax.dynamic_slice_in_dim(potential, (me % half) * na, na, 1)

    block = pl.BlockSpec((ch, ch), lambda m, s, *_: (m, s))
    hi, lo = pl.pallas_call(
        functools.partial(coupling_kernel, cb),
        out_shape=[sds((lam * ch, 2 * ch), BF16)] * 2,
        grid_spec=pltpu.PrefetchScalarGridSpec(
            num_scalar_prefetch=2,
            grid=(lam, 2),
            in_specs=[pl.BlockSpec((1, ch, ch), lambda m, s, side, pat: (m, side[0], (side[0] + s) % 2))],
            out_specs=[block, block],
        ),
        cost_estimate=pl.CostEstimate(flops=0, bytes_accessed=1 << 16, transcendentals=0),
    )(side, pattern, angular)
    hi, lo = local(hi), local(lo)

    piece = pltpu.VMEM((na * nc, nb), F32)
    last_piece = pltpu.VMEM((na * nc + 8, nb), F32)
    packed = pltpu.VMEM((half, nk * nc, nb), F32)
    square = pltpu.VMEM((8, nb), F32)
    y_scratch = pltpu.VMEM((min(8, nc), nr, nb), F32)
    natural = sds((nc, nr, nb), F32)

    def kinetic(prev, cur=None, pieces=(), out=None):
        outs = [piece] * half + ([out] if pieces else [])
        arrays = [ks2, kr2, rot, orb, prev] + (list(pieces) if pieces else [cur])
        res = call(
            functools.partial(kinetic_kernel, na, nc, len(pieces), half), outs, [spot, quanta], arrays, [y_scratch]
        )
        return res if pieces else (*res, None)

    def mix(u, own, oth, q, early=(), norms=()):
        last = q == n_chunk - 1
        final = bool(norms)
        outs = ([] if final and last else [packed]) + ([] if final and last else [square])
        outs += [last_piece if final else piece] * half if last else []
        keep = not (final and last)
        return call(
            functools.partial(mix_kernel, lam, nc, q, half, len(early), len(norms) if last else 0, keep, last),
            outs,
            [spot],
            [hi, lo, pot2, own, oth, *u, *early, *(norms if last else ())],
            [] if keep else [packed],
        )

    def step(u, own, oth, norms=()):
        chunks, squares = [], []
        for q in range(n_chunk):
            last = q == n_chunk - 1
            seen = (*norms, *squares) if norms else ()
            res = mix(u, own[q], oth[q], q, chunks if last else (), seen)
            if norms and last:
                return res
            chunks.append(res[0])
            squares.append(res[1])
        return chunks, res[2:], squares

    pieces = call(functools.partial(to_pieces_kernel, na, nc), [piece] * half, [spot], [psi_cur])
    v1 = call(functools.partial(pack_kernel, half), [packed] * n_chunk, [spot], exchange(pieces))
    o1 = [local(swap(x)) for x in v1]
    u1 = exchange(kinetic(psi_prev, cur=psi_cur)[:-1])
    v2, pieces, s2 = step(u1, v1, o1)
    o2 = [local(swap(x)) for x in v2]
    *u2, v2_nat = kinetic(psi_cur, pieces=exchange(pieces), out=pltpu.VMEM((nc, nr, nb), F32))
    v3, pieces, s3 = step(exchange(u2), v2, o2)
    o3 = [local(swap(x)) for x in v3]
    *u3, prev_out = kinetic(v2_nat, pieces=exchange(pieces), out=natural)
    pieces = step(exchange(u3), v3, o3, (*s2, *s3))
    cur_out, sums = call(
        functools.partial(finish_kernel, na, nc, half),
        [natural, pltpu.VMEM((8, nb), F32)],
        [spot],
        exchange(pieces),
        [pltpu.VMEM((half, 8, nb), F32)],
    )
    sums = sums + swap(sums)
    norms = jnp.sum(sums[:ITERS], axis=1) / (total_ch * nr * nb)
    return prev_out, cur_out, norms


def solution(mesh):
    return jax.shard_map(
        per_device,
        mesh=mesh,
        in_specs=(
            P(("groups", "chan"), None, None),
            P(("groups", "chan"), None, None),
            P(),
            P(),
            P(),
            P("groups", None, None),
            P("groups", None),
            P(("groups", "chan"), None),
        ),
        out_specs=(
            P(("groups", "chan"), None, None),
            P(("groups", "chan"), None, None),
            P("groups"),
        ),
        check_vma=False,
    )
```

```python
import functools

import jax
import jax.numpy as jnp
import numpy as np
from jax import lax
from jax.experimental import pallas as pl
from jax.experimental.pallas import tpu as pltpu
from jax.sharding import PartitionSpec as P

JL_MAX = 40
ITERS = 3
TEAM = 4
F32 = jnp.float32
BF16 = jnp.bfloat16
HP = lax.Precision.HIGHEST
VM = pl.BlockSpec(memory_space=pltpu.VMEM)
SM = pl.BlockSpec(memory_space=pltpu.SMEM)
ANY = pl.BlockSpec(memory_space=pl.ANY)


def place(me_ref):
    return me_ref[0] // TEAM, me_ref[0] % TEAM


def rows_of(spot, s, q, na, nk):
    return pl.ds(pl.multiple_of((spot ^ s) * na + q * nk, nk), nk)


def to_pieces_kernel(na, nc, n, n_chunk, me_ref, x_ref, *outs):
    spot, _ = place(me_ref)
    nk = na // n_chunk
    for q in range(n_chunk):
        for s in range(n):
            out = outs[q * n + s]
            for c in range(nc):
                out[pl.ds(c, nk, stride=nc), :] = x_ref[c, rows_of(spot, s, q, na, nk), :]


def pack_kernel(n, me_ref, *refs):
    spot, _ = place(me_ref)
    for s in range(n):
        refs[n][spot ^ s] = refs[s][...]


def kinetic_kernel(na, nc, n, n_chunk, from_pieces, to_pieces, me_ref, quanta, ks, kr, prev, *refs):
    spot, _ = place(me_ref)
    nk = na // n_chunk
    refs = list(refs)
    take = lambda k: [refs.pop(0) for _ in range(k)]
    pieces = take(n * n_chunk) if from_pieces else ()
    cur = None if from_pieces else take(1)[0]
    u_refs = take(n * n_chunk if to_pieces else 1)
    cur = take(1)[0] if from_pieces else cur
    y_ref = refs.pop(0) if to_pieces else u_refs[0]
    nr, nb = prev.shape[1:]
    kstr = 2.0 * ks[...]
    krad = 2.0 * kr[...]
    stretch = 1.0 + lax.broadcasted_iota(jnp.int32, (nr, nb), 0).astype(F32) / nr
    radius = 1.0 + 3.0 * lax.broadcasted_iota(jnp.int32, (nr, nb), 1).astype(F32) / nb
    rotation = 1.0 / (stretch * stretch)
    orbital = 1.0 / (radius * radius)
    scale = np.float32(0.3 / (JL_MAX * (JL_MAX - 1)))
    group = min(8, nc)
    for start in range(0, nc, group):
        chans = range(start, start + group)
        if from_pieces:
            for q in range(n_chunk):
                for s in range(n):
                    for c in chans:
                        cur[c, rows_of(spot, s, q, na, nk), :] = pieces[q * n + s][pl.ds(c, nk, stride=nc), :]
        tiles = [cur[c] for c in chans]
        mixed_a = jnp.dot(kstr, jnp.concatenate(tiles, 1), precision=HP, preferred_element_type=F32)
        mixed_b = jnp.dot(jnp.concatenate(tiles, 0), krad, precision=HP, preferred_element_type=F32)
        for i, c in enumerate(chans):
            j = quanta[c, 0].astype(F32)
            l = quanta[c, 1].astype(F32)
            barrier = orbital * (scale * (l * (l + 1.0))) + rotation * (scale * (j * (j + 1.0))) - 0.2
            y = mixed_a[:, i * nb : (i + 1) * nb] + mixed_b[i * nr : (i + 1) * nr]
            y_ref[i if to_pieces else c] = y + barrier * tiles[i] - prev[c]
        if to_pieces:
            for q in range(n_chunk):
                for s in range(n):
                    for i, c in enumerate(chans):
                        u_refs[q * n + s][pl.ds(c, nk, stride=nc), :] = y_ref[i, rows_of(spot, s, q, na, nk), :]


def coupling_kernel(cb, nc, n, me_ref, pat_ref, ang_ref, out_ref, buf, sems):
    _, seat = place(me_ref)
    lam, _, tot = ang_ref.shape

    def row(z):
        return (z * TEAM + seat) * nc

    copies = [
        pltpu.make_async_copy(
            ang_ref.at[m, pl.ds(pl.multiple_of(row(z), nc), nc), :], buf.at[m, z], sems.at[m * n + z]
        )
        for m in range(lam)
        for z in range(n)
    ]
    for copy in copies:
        copy.start()
    lane = lax.broadcasted_iota(jnp.int32, (nc, tot), 1) // cb
    for copy in copies:
        copy.wait()
    for z in range(n):
        factor = jnp.zeros((nc, tot), F32)
        for k in range(tot // cb):
            factor = jnp.where(lane == k, pat_ref[row(z) // cb, k].astype(F32), factor)
        for m in range(lam):
            val = buf[m, z] * factor
            hi = val.astype(BF16)
            out_ref[m, 0, z] = hi
            out_ref[m, 1, z] = (val - hi.astype(F32)).astype(BF16)


def mix_kernel(nc, q, n, mode, me_ref, coup, pot, *refs):
    spot, seat = place(me_ref)
    sources, refs = refs[:TEAM], list(refs[TEAM:])
    take = lambda k: [refs.pop(0) for _ in range(k)]
    us = take(n) if mode == "next" else ()
    pieces = take(n)
    out, sq = take(2) if mode == "next" else (None, None)
    tmp = out if mode == "next" else refs.pop(0)
    xs_hi, xs_lo = refs
    _, rows, nb = sources[0].shape
    nk, ch = rows // nc, n * nc
    lam, tot = coup.shape[0], coup.shape[-1]
    for m, src in enumerate(sources):
        for z in range(n):
            x = jnp.concatenate([src[z, k * nc : (k + 1) * nc] for k in range(nk)], 1)
            hi = x.astype(BF16)
            xs_hi[z * TEAM + (seat ^ m)] = hi
            xs_lo[z * TEAM + (seat ^ m)] = (x - hi.astype(F32)).astype(BF16)
    for s, u in enumerate(us):
        tmp[spot ^ s] = u[...]
    x_hi = xs_hi[...].reshape(tot, nk * nb)
    x_lo = xs_lo[...].reshape(tot, nk * nb)
    na = pot.shape[1] // n
    acc = None
    for m in range(lam):
        both = coup[m].reshape(2 * ch, tot)
        p = jnp.dot(both, x_hi, preferred_element_type=F32)
        p = p[:ch] + p[ch:] + jnp.dot(both[:ch], x_lo, preferred_element_type=F32)
        w = jnp.concatenate([pot[m, pl.ds(spot * na + q * nk + k, 1), :] for k in range(nk)], 1)
        p = p * (2.0 * w)
        acc = p if acc is None else acc + p
    total = jnp.zeros((8, nb), F32)
    for k in range(nk):
        y = acc[:, k * nb : (k + 1) * nb].reshape(n, nc, nb)
        if mode == "next":
            y = y + tmp[:, k * nc : (k + 1) * nc]
            total = total + jnp.sum((y * y).reshape(ch // 8, 8, nb), axis=0)
        tmp[:, k * nc : (k + 1) * nc] = y
    for s, piece in enumerate(pieces):
        piece[...] = tmp[spot ^ s]
    if mode == "next":
        sq[...] = total


def finish_kernel(na, nc, n, n_chunk, me_ref, u_ref, *refs):
    spot, _ = place(me_ref)
    nk = na // n_chunk
    pieces, squares, (out, sums) = refs[: n * n_chunk], refs[n * n_chunk : -2], refs[-2:]
    nb = u_ref.shape[-1]
    total = jnp.zeros((nk, nb), F32)
    for q in range(n_chunk):
        for s in range(n):
            at = rows_of(spot, s, q, na, nk)
            for c in range(nc):
                y = u_ref[c, at, :] + pieces[q * n + s][pl.ds(c, nk, stride=nc), :]
                out[c, at, :] = y
                total = total + y * y
    tiles = [sum((r[...] for r in squares[k + 1 : k + n_chunk]), squares[k][...]) for k in (0, n_chunk)]
    tiles = [jnp.sum(t, axis=0, keepdims=True) for t in (*tiles, total)]
    sums[...] = jnp.concatenate([*tiles, jnp.zeros((8 - ITERS, nb), F32)], 0)


def local(x):
    return pltpu.with_memory_space_constraint(x, pltpu.VMEM)


def call(kernel, outs, scalars, arrays, scratch=(), specs=None):
    return pl.pallas_call(
        kernel,
        out_shape=outs,
        in_specs=[SM] * len(scalars) + (specs or [VM] * len(arrays)),
        out_specs=[VM] * len(outs),
        scratch_shapes=list(scratch),
        compiler_params=pltpu.CompilerParams(vmem_limit_bytes=20 << 20),
        cost_estimate=pl.CostEstimate(flops=0, bytes_accessed=1 << 16, transcendentals=0),
    )(*scalars, *arrays)


def per_device(psi_prev, psi_cur, kin_stretch, kin_radius, potential, angular, pattern, quanta):
    nc, nr, nb = psi_cur.shape
    lam = potential.shape[0]
    nd = lax.axis_size("chan")
    n = nd // TEAM
    na = nr // n
    total_ch = nc * nd
    cb = total_ch // pattern.shape[1]
    n_chunk = 2 if na % 2 == 0 else 1
    nk = na // n_chunk
    me = lax.axis_index("chan").astype(jnp.int32).reshape(1)
    sds = jax.ShapeDtypeStruct

    def swap(x, bits):
        return lax.ppermute(x, "chan", [(i, i ^ bits) for i in range(nd)])

    def across(x, bits):
        return local(swap(x, bits))

    def exchange(pieces):
        return [across(x, i % n * TEAM) if i % n else x for i, x in enumerate(pieces)]

    def gather(x):
        over = across(x, 2)
        return [x, across(x, 1), over, across(over, 1)]

    piece = pltpu.VMEM((nk * nc, nb), F32)
    packed = pltpu.VMEM((n, nk * nc, nb), F32)
    square = pltpu.VMEM((8, nb), F32)
    on_chip = pltpu.VMEM((nc, nr, nb), F32)
    natural = sds((nc, nr, nb), F32)
    shape = (na, nc, n, n_chunk)

    (coup,) = call(
        functools.partial(coupling_kernel, cb, nc, n),
        [pltpu.VMEM((lam, 2, n, nc, total_ch), BF16)],
        [me, pattern],
        [angular],
        [pltpu.VMEM((lam, n, nc, total_ch), F32), pltpu.SemaphoreType.DMA((lam * n,))],
        [ANY],
    )

    def kinetic(prev, cur, from_pieces, to_pieces, out=None):
        outs = ([piece] * (n * n_chunk) if to_pieces else [on_chip]) + ([out] if from_pieces else [])
        scratch = [pltpu.VMEM((min(8, nc), nr, nb), F32)] if to_pieces else []
        kernel = functools.partial(kinetic_kernel, *shape, from_pieces, to_pieces)
        return call(kernel, outs, [me, quanta], [kin_stretch, kin_radius, prev, *cur], scratch)

    def mix(q, sources, u=()):
        keep = bool(u)
        outs = [piece] * n + ([packed, square] if keep else [])
        split = pltpu.VMEM((nd, nc, nk * nb), BF16)
        return call(
            functools.partial(mix_kernel, nc, q, n, "next" if keep else "last"),
            outs,
            [me],
            [coup, potential, *sources, *u],
            ([] if keep else [packed]) + [split, split],
        )

    def step(v, u):
        pieces, chunks, squares = [], [], []
        for q in range(n_chunk):
            *part, chunk, square_sum = mix(q, gather(v[q]), u[q * n : (q + 1) * n])
            pieces += part
            chunks.append(chunk)
            squares.append(square_sum)
        return exchange(pieces), chunks, squares

    pieces = exchange(
        call(functools.partial(to_pieces_kernel, *shape), [piece] * (n * n_chunk), [me], [psi_cur])
    )
    v1 = [
        call(functools.partial(pack_kernel, n), [packed], [me], pieces[q * n : (q + 1) * n])[0]
        for q in range(n_chunk)
    ]
    u1 = exchange(kinetic(psi_prev, [psi_cur], False, True))
    pieces, v2, s2 = step(v1, u1)
    *u2, v2_nat = kinetic(psi_cur, pieces, True, True, on_chip)
    pieces, v3, s3 = step(v2, exchange(u2))
    u3, prev_out = kinetic(v2_nat, pieces, True, False, natural)
    pieces = exchange([p for q in range(n_chunk) for p in mix(q, gather(v3[q]))])
    cur_out, sums = call(
        functools.partial(finish_kernel, *shape), [natural, sds((8, nb), F32)], [me], [u3, *pieces, *s2, *s3]
    )
    bit = 1
    while bit < nd:
        sums = (sums + swap(sums, bit)) + (swap(sums, 2 * bit) + swap(sums, 3 * bit))
        bit *= 4
    norms = jnp.sum(sums[:ITERS], axis=1) / (total_ch * nr * nb)
    return prev_out, cur_out, norms


def solution(mesh):
    return jax.shard_map(
        per_device,
        mesh=mesh,
        in_specs=(
            P(("groups", "chan"), None, None),
            P(("groups", "chan"), None, None),
            P(),
            P(),
            P(),
            P("groups", None, None),
            P("groups", None),
            P(("groups", "chan"), None),
        ),
        out_specs=(
            P(("groups", "chan"), None, None),
            P(("groups", "chan"), None, None),
            P("groups"),
        ),
        check_vma=False,
    )
```

```python
import functools

import jax
import jax.numpy as jnp
import numpy as np
from jax import lax
from jax.experimental import pallas as pl
from jax.experimental.pallas import tpu as pltpu
from jax.sharding import PartitionSpec as P

JL_MAX = 40
ITERS = 3
TEAM = 4
F32 = jnp.float32
BF16 = jnp.bfloat16
HP = lax.Precision.HIGHEST
VM = pl.BlockSpec(memory_space=pltpu.VMEM)
SM = pl.BlockSpec(memory_space=pltpu.SMEM)
ANY = pl.BlockSpec(memory_space=pl.ANY)


def place(me_ref):
    return me_ref[0] // TEAM, me_ref[0] % TEAM


def rows_of(spot, s, na):
    return pl.ds(pl.multiple_of((spot ^ s) * na, na), na)


def to_pieces_kernel(na, nc, me_ref, x_ref, *outs):
    spot, _ = place(me_ref)
    for s, out in enumerate(outs):
        for c in range(nc):
            out[pl.ds(c, na, stride=nc), :] = x_ref[c, rows_of(spot, s, na), :]


def pack_kernel(n, me_ref, *refs):
    spot, _ = place(me_ref)
    for s in range(n):
        refs[-1][spot ^ s] = refs[s][...]


def kinetic_kernel(na, nc, n, from_pieces, to_pieces, me_ref, quanta, ks, kr, prev, *refs):
    spot, _ = place(me_ref)
    refs = list(refs)
    take = lambda k: [refs.pop(0) for _ in range(k)]
    pieces = take(n) if from_pieces else ()
    cur = None if from_pieces else take(1)[0]
    u_refs = take(n if to_pieces else 1)
    cur = take(1)[0] if from_pieces else cur
    y_ref = refs.pop(0) if to_pieces else u_refs[0]
    nr, nb = prev.shape[1:]
    kstr = 2.0 * ks[...]
    krad = 2.0 * kr[...]
    stretch = 1.0 + lax.broadcasted_iota(jnp.int32, (nr, nb), 0).astype(F32) / nr
    radius = 1.0 + 3.0 * lax.broadcasted_iota(jnp.int32, (nr, nb), 1).astype(F32) / nb
    rotation = 1.0 / (stretch * stretch)
    orbital = 1.0 / (radius * radius)
    scale = np.float32(0.3 / (JL_MAX * (JL_MAX - 1)))
    group = min(8, nc)
    for start in range(0, nc, group):
        chans = range(start, start + group)
        for s, piece in enumerate(pieces):
            for c in chans:
                cur[c, rows_of(spot, s, na), :] = piece[pl.ds(c, na, stride=nc), :]
        tiles = [cur[c] for c in chans]
        mixed_a = jnp.dot(kstr, jnp.concatenate(tiles, 1), precision=HP, preferred_element_type=F32)
        mixed_b = jnp.dot(jnp.concatenate(tiles, 0), krad, precision=HP, preferred_element_type=F32)
        for i, c in enumerate(chans):
            j = quanta[c, 0].astype(F32)
            l = quanta[c, 1].astype(F32)
            barrier = orbital * (scale * (l * (l + 1.0))) + rotation * (scale * (j * (j + 1.0))) - 0.2
            y = mixed_a[:, i * nb : (i + 1) * nb] + mixed_b[i * nr : (i + 1) * nr]
            y_ref[i if to_pieces else c] = y + barrier * tiles[i] - prev[c]
        if to_pieces:
            for s, u in enumerate(u_refs):
                for i, c in enumerate(chans):
                    u[pl.ds(c, na, stride=nc), :] = y_ref[i, rows_of(spot, s, na), :]


def coupling_kernel(cb, nc, n, me_ref, pat_ref, ang_ref, out_ref, buf, sems):
    _, seat = place(me_ref)
    lam, _, tot = ang_ref.shape

    def row(z):
        return (z * TEAM + seat) * nc

    copies = [
        pltpu.make_async_copy(
            ang_ref.at[m, pl.ds(pl.multiple_of(row(z), nc), nc), :], buf.at[m, z], sems.at[m * n + z]
        )
        for m in range(lam)
        for z in range(n)
    ]
    for copy in copies:
        copy.start()
    lane = lax.broadcasted_iota(jnp.int32, (nc, tot), 1) // cb
    for copy in copies:
        copy.wait()
    for z in range(n):
        factor = jnp.zeros((nc, tot), F32)
        for k in range(tot // cb):
            factor = jnp.where(lane == k, pat_ref[row(z) // cb, k].astype(F32), factor)
        for m in range(lam):
            val = buf[m, z] * factor
            hi = val.astype(BF16)
            out_ref[m, 0, z] = hi
            out_ref[m, 1, z] = (val - hi.astype(F32)).astype(BF16)


def mix_kernel(nc, n, mode, me_ref, coup, pot, *refs):
    spot, seat = place(me_ref)
    sources, refs = refs[:TEAM], list(refs[TEAM:])
    take = lambda k: [refs.pop(0) for _ in range(k)]
    us = take(n) if mode == "next" else ()
    pieces = take(n) if mode != "part" else ()
    tmp = refs.pop(0)
    sq = refs.pop(0) if mode == "next" else None
    xs_hi, xs_lo = refs
    _, rows, nb = sources[0].shape
    na, ch = rows // nc, n * nc
    lam, tot = coup.shape[0], coup.shape[-1]
    step = max(1, na // 2)
    for s, u in enumerate(us):
        tmp[spot ^ s] = u[...]
    total = jnp.zeros((8, nb), F32)
    for k0 in range(0, na, step):
        ks = range(k0, k0 + step)
        for m, src in enumerate(sources):
            for z in range(n):
                x = jnp.concatenate([src[z, k * nc : (k + 1) * nc] for k in ks], 1)
                hi = x.astype(BF16)
                xs_hi[z * TEAM + (seat ^ m)] = hi
                xs_lo[z * TEAM + (seat ^ m)] = (x - hi.astype(F32)).astype(BF16)
        x_hi = xs_hi[...].reshape(tot, step * nb)
        x_lo = xs_lo[...].reshape(tot, step * nb)
        acc = None
        for m in range(lam):
            both = coup[m].reshape(2 * ch, tot)
            p = jnp.dot(both, x_hi, preferred_element_type=F32)
            p = p[:ch] + p[ch:] + jnp.dot(both[:ch], x_lo, preferred_element_type=F32)
            w = jnp.concatenate([pot[m, pl.ds(spot * na + k, 1), :] for k in ks], 1)
            p = p * (2.0 * w)
            acc = p if acc is None else acc + p
        for i, k in enumerate(ks):
            y = acc[:, i * nb : (i + 1) * nb].reshape(n, nc, nb)
            if mode == "next":
                y = y + tmp[:, k * nc : (k + 1) * nc]
                total = total + jnp.sum((y * y).reshape(ch // 8, 8, nb), axis=0)
            tmp[:, k * nc : (k + 1) * nc] = y
    for s, piece in enumerate(pieces):
        piece[...] = tmp[spot ^ s]
    if mode == "next":
        sq[...] = total


def join_kernel(n, me_ref, w_ref, *refs):
    spot, _ = place(me_ref)
    us, pieces, (out, sq) = refs[:n], refs[n:-2], refs[-2:]
    nb = w_ref.shape[-1]
    total = jnp.zeros((8, nb), F32)
    for s in range(n):
        y = w_ref[spot ^ s] + us[s][...]
        out[spot ^ s] = y
        pieces[s][...] = y
        total = total + jnp.sum((y * y).reshape(-1, 8, nb), axis=0)
    sq[...] = total


def last_of(na, nc, u_ref, pieces, spot):
    for s, piece in enumerate(pieces):
        at = rows_of(spot, s, na)
        for c in range(nc):
            yield c, at, u_ref[c, at, :] + piece[pl.ds(c, na, stride=nc), :]


def norm_kernel(na, nc, me_ref, s2_ref, s3_ref, u_ref, *refs):
    spot, _ = place(me_ref)
    nb = u_ref.shape[-1]
    total = jnp.zeros((na, nb), F32)
    for _, _, y in last_of(na, nc, u_ref, refs[:-1], spot):
        total = total + y * y
    tiles = [jnp.sum(t, axis=0, keepdims=True) for t in (s2_ref[...], s3_ref[...], total)]
    refs[-1][...] = jnp.concatenate([*tiles, jnp.zeros((8 - ITERS, nb), F32)], 0)


def finish_kernel(na, nc, me_ref, u_ref, *refs):
    spot, _ = place(me_ref)
    for c, at, y in last_of(na, nc, u_ref, refs[:-1], spot):
        refs[-1][c, at, :] = y


def local(x):
    return pltpu.with_memory_space_constraint(x, pltpu.VMEM)


def call(kernel, outs, scalars, arrays, scratch=(), specs=None):
    return pl.pallas_call(
        kernel,
        out_shape=outs,
        in_specs=[SM] * len(scalars) + (specs or [VM] * len(arrays)),
        out_specs=[VM] * len(outs),
        scratch_shapes=list(scratch),
        compiler_params=pltpu.CompilerParams(vmem_limit_bytes=20 << 20),
        cost_estimate=pl.CostEstimate(flops=0, bytes_accessed=1 << 16, transcendentals=0),
    )(*scalars, *arrays)


def per_device(psi_prev, psi_cur, kin_stretch, kin_radius, potential, angular, pattern, quanta):
    nc, nr, nb = psi_cur.shape
    lam = potential.shape[0]
    nd = lax.axis_size("chan")
    n = nd // TEAM
    na = nr // n
    total_ch = nc * nd
    cb = total_ch // pattern.shape[1]
    me = lax.axis_index("chan").astype(jnp.int32).reshape(1)
    sds = jax.ShapeDtypeStruct

    def swap(x, bits):
        return lax.ppermute(x, "chan", [(i, i ^ bits) for i in range(nd)])

    def across(x, bits):
        return local(swap(x, bits))

    def exchange(pieces):
        return [across(x, s * TEAM) if s else x for s, x in enumerate(pieces)]

    def gather(x, first):
        over = lax.optimization_barrier((swap(x, 2), *first))[0]
        return [x, across(x, 1), local(over), across(over, 1)]

    piece = pltpu.VMEM((na * nc, nb), F32)
    packed = pltpu.VMEM((n, na * nc, nb), F32)
    square = pltpu.VMEM((8, nb), F32)
    on_chip = pltpu.VMEM((nc, nr, nb), F32)
    natural = sds((nc, nr, nb), F32)
    split = pltpu.VMEM((nd, nc, max(1, na // 2) * nb), BF16)

    def kinetic(prev, cur, from_pieces, to_pieces, out=None):
        outs = ([piece] * n if to_pieces else [on_chip]) + ([out] if from_pieces else [])
        scratch = [pltpu.VMEM((min(8, nc), nr, nb), F32)] if to_pieces else []
        kernel = functools.partial(kinetic_kernel, na, nc, n, from_pieces, to_pieces)
        return call(kernel, outs, [me, quanta], [kin_stretch, kin_radius, prev, *cur], scratch)

    def mix(mode, v, beside, u=()):
        outs = [] if mode == "part" else [piece] * n
        outs += [] if mode == "last" else [packed]
        outs += [square] if mode == "next" else []
        scratch = ([packed] if mode == "last" else []) + [split, split]
        return call(
            functools.partial(mix_kernel, nc, n, mode), outs, [me], [coup, potential, *gather(v, beside), *u], scratch
        )

    (coup,) = call(
        functools.partial(coupling_kernel, cb, nc, n),
        [pltpu.VMEM((lam, 2, n, nc, total_ch), BF16)],
        [me, pattern],
        [angular],
        [pltpu.VMEM((lam, n, nc, total_ch), F32), pltpu.SemaphoreType.DMA((lam * n,))],
        [pl.BlockSpec(memory_space=pltpu.HBM)],
    )
    pieces = exchange(call(functools.partial(to_pieces_kernel, na, nc), [piece] * n, [me], [psi_cur]))
    u1 = kinetic(psi_prev, [psi_cur], False, True)
    (v1,) = call(
        functools.partial(pack_kernel, n), [packed], [me], [*pieces, coup, u1[0]], (), [VM] * n + [ANY] * 2
    )
    u1 = exchange(u1)
    *pieces, v2, s2 = mix("next", v1, u1[1:], u1)
    pieces = exchange(pieces)
    *u2, v2_nat = kinetic(psi_cur, pieces, True, True, on_chip)
    (w2,) = mix("part", v2, pieces[1:])
    *pieces, v3, s3 = call(
        functools.partial(join_kernel, n), [piece] * n + [packed, square], [me], [w2, *exchange(u2)]
    )
    pieces = exchange(pieces)
    u3, prev_out = kinetic(v2_nat, pieces, True, False, natural)
    pieces = exchange(mix("last", v3, pieces[1:]))
    (sums,) = call(functools.partial(norm_kernel, na, nc), [sds((8, nb), F32)], [me], [s2, s3, u3, *pieces])
    (cur_out,) = call(functools.partial(finish_kernel, na, nc), [natural], [me], [u3, *pieces])
    bit = 1
    while bit < nd:
        sums = (sums + swap(sums, bit)) + (swap(sums, 2 * bit) + swap(sums, 3 * bit))
        bit *= 4
    norms = jnp.sum(sums[:ITERS], axis=1) / (total_ch * nr * nb)
    return prev_out, cur_out, norms


def solution(mesh):
    return jax.shard_map(
        per_device,
        mesh=mesh,
        in_specs=(
            P(("groups", "chan"), None, None),
            P(("groups", "chan"), None, None),
            P(),
            P(),
            P(),
            P("groups", None, None),
            P("groups", None),
            P(("groups", "chan"), None),
        ),
        out_specs=(
            P(("groups", "chan"), None, None),
            P(("groups", "chan"), None, None),
            P("groups"),
        ),
        check_vma=False,
    )
```

```python
import functools

import jax
import jax.numpy as jnp
import numpy as np
from jax import lax
from jax.experimental import pallas as pl
from jax.experimental.pallas import tpu as pltpu
from jax.sharding import PartitionSpec as P

JL_MAX = 40
ITERS = 3
TEAM = 4
F32 = jnp.float32
BF16 = jnp.bfloat16
HP = lax.Precision.HIGHEST
VM = pl.BlockSpec(memory_space=pltpu.VMEM)
SM = pl.BlockSpec(memory_space=pltpu.SMEM)
ANY = pl.BlockSpec(memory_space=pl.ANY)


def hop(i, n):
    return i % (n - 1) + 1 if i else 0


def place(me_ref):
    return me_ref[0] // TEAM, me_ref[0] % TEAM


def rows_of(spot, s, n, na):
    return pl.ds(pl.multiple_of((spot ^ hop(s, n)) * na, na), na)


def to_pieces_kernel(na, nc, me_ref, x_ref, *outs):
    spot, _ = place(me_ref)
    for s, out in enumerate(outs):
        for c in range(nc):
            out[pl.ds(c, na, stride=nc), :] = x_ref[c, rows_of(spot, s, len(outs), na), :]


def kinetic_kernel(na, nc, n, n_in, based, n_out, me_ref, quanta, ks, kr, prev, *refs):
    spot, _ = place(me_ref)
    refs = list(refs)
    take = lambda k: [refs.pop(0) for _ in range(k)]
    pieces = take(n_in)
    base = refs.pop(0) if based else None
    cur = None if n_in else refs.pop(0)
    u_refs = take(n_out)
    y_ref = refs.pop(0)
    cur = refs.pop(0) if n_in else cur
    nr, nb = prev.shape[1:]
    kstr = 2.0 * ks[...]
    krad = 2.0 * kr[...]
    stretch = 1.0 + lax.broadcasted_iota(jnp.int32, (nr, nb), 0).astype(F32) / nr
    radius = 1.0 + 3.0 * lax.broadcasted_iota(jnp.int32, (nr, nb), 1).astype(F32) / nb
    rotation = 1.0 / (stretch * stretch)
    orbital = 1.0 / (radius * radius)
    scale = np.float32(0.3 / (JL_MAX * (JL_MAX - 1)))
    group = min(8, nc)
    for start in range(0, nc, group):
        chans = range(start, start + group)
        for s, piece in enumerate(pieces):
            for c in chans:
                at = rows_of(spot, s, n, na)
                x = piece[pl.ds(c, na, stride=nc), :]
                cur[c, at, :] = x + base[c, at, :] if based else x
        tiles = [cur[c] for c in chans]
        mixed_a = jnp.dot(kstr, jnp.concatenate(tiles, 1), precision=HP, preferred_element_type=F32)
        mixed_b = jnp.dot(jnp.concatenate(tiles, 0), krad, precision=HP, preferred_element_type=F32)
        for i, c in enumerate(chans):
            j = quanta[c, 0].astype(F32)
            l = quanta[c, 1].astype(F32)
            barrier = orbital * (scale * (l * (l + 1.0))) + rotation * (scale * (j * (j + 1.0))) - 0.2
            y = mixed_a[:, i * nb : (i + 1) * nb] + mixed_b[i * nr : (i + 1) * nr]
            y_ref[c] = y + barrier * tiles[i] - prev[c]
        for s, u in enumerate(u_refs):
            for c in chans:
                u[pl.ds(c, na, stride=nc), :] = y_ref[c, rows_of(spot, s, n, na), :]


def coupling_kernel(cb, nc, n, me_ref, pat_ref, ang_ref, out_ref, buf, sems):
    spot, seat = place(me_ref)
    lam, _, tot = ang_ref.shape

    def row(s):
        return ((spot ^ hop(s, n)) * TEAM + seat) * nc

    copies = [
        pltpu.make_async_copy(
            ang_ref.at[m, pl.ds(pl.multiple_of(row(z), nc), nc), :], buf.at[m, z], sems.at[m * n + z]
        )
        for m in range(lam)
        for z in range(n)
    ]
    for copy in copies:
        copy.start()
    lane = lax.broadcasted_iota(jnp.int32, (nc, tot), 1) // cb
    for copy in copies:
        copy.wait()
    for z in range(n):
        factor = jnp.zeros((nc, tot), F32)
        for k in range(tot // cb):
            factor = jnp.where(lane == k, pat_ref[row(z) // cb, k].astype(F32), factor)
        for m in range(lam):
            val = buf[m, z] * factor
            hi = val.astype(BF16)
            out_ref[m, 0, z] = hi
            out_ref[m, 1, z] = (val - hi.astype(F32)).astype(BF16)


def mix_kernel(nc, n, n_ref, me_ref, coup, pot, *refs):
    spot, seat = place(me_ref)
    sources, pieces = refs[: TEAM * n_ref], refs[TEAM * n_ref : -2]
    xs_hi, xs_lo = refs[-2:]
    rows, nb = pieces[0].shape
    na, ch = rows // nc, n * nc
    lam, tot = coup.shape[0], coup.shape[-1]
    step = max(1, na // 2)
    for k0 in range(0, na, step):
        ks = range(k0, k0 + step)
        for m in range(TEAM):
            for s in range(n):
                if n_ref == 1:
                    z, src = s, sources[m].at[s]
                else:
                    far = s % (n - 1) > 0
                    z, src = spot ^ hop(s, n), sources[m * 2 + (not far)].at[s - 1 if far else s // (n - 1)]
                x = jnp.concatenate([src[k * nc : (k + 1) * nc] for k in ks], 1)
                hi = x.astype(BF16)
                xs_hi[z * TEAM + (seat ^ m)] = hi
                xs_lo[z * TEAM + (seat ^ m)] = (x - hi.astype(F32)).astype(BF16)
        x_hi = xs_hi[...].reshape(tot, step * nb)
        x_lo = xs_lo[...].reshape(tot, step * nb)
        acc = None
        for m in range(lam):
            both = coup[m].reshape(2 * ch, tot)
            p = jnp.dot(both, x_hi, preferred_element_type=F32)
            p = p[:ch] + p[ch:] + jnp.dot(both[:ch], x_lo, preferred_element_type=F32)
            w = jnp.concatenate([pot[m, pl.ds(spot * na + k, 1), :] for k in ks], 1)
            p = p * (2.0 * w)
            acc = p if acc is None else acc + p
        for s, piece in enumerate(pieces):
            for i, k in enumerate(ks):
                piece[k * nc : (k + 1) * nc] = acc[s * nc : (s + 1) * nc, i * nb : (i + 1) * nb]


def near_far(pieces):
    return [pieces[0], pieces[-1]], pieces[1:-1]


def join_kernel(where, n_add, n_out, n_behind, me_ref, *refs):
    spot, _ = place(me_ref)
    n = len(where)
    terms = [refs[k * n : (k + 1) * n] for k in range(n_add)]
    packed, outs, sq = refs[n_add * n + n_behind], refs[n_add * n + n_behind + 1 :][:n_out], refs[-1]
    total = 0.0
    for i, at in enumerate(where):
        y = sum((t[i][...] for t in terms[1:]), terms[0][i][...])
        packed[i if at is None else spot ^ at] = y
        if n_out:
            outs[i][...] = y
        if n_add > 1:
            total = total + jnp.sum((y * y).reshape(-1, 8, y.shape[1]), axis=0)
    if n_add > 1:
        sq[...] = total


def last_of(na, nc, u_ref, pieces, spot):
    for s, piece in enumerate(pieces):
        at = rows_of(spot, s, len(pieces), na)
        for c in range(nc):
            yield c, at, u_ref[c, at, :] + piece[pl.ds(c, na, stride=nc), :]


def norm_kernel(na, nc, n, me_ref, u_ref, *refs):
    spot, _ = place(me_ref)
    nb = u_ref.shape[-1]
    total = jnp.zeros((na, nb), F32)
    for _, _, y in last_of(na, nc, u_ref, refs[:n], spot):
        total = total + y * y
    squares = [r[...] for r in refs[n:-1]]
    tiles = [jnp.sum(t, axis=0, keepdims=True) for t in (squares[0], sum(squares[2:], squares[1]), total)]
    refs[-1][...] = jnp.concatenate([*tiles, jnp.zeros((8 - ITERS, nb), F32)], 0)


def finish_kernel(na, nc, me_ref, u_ref, *refs):
    spot, _ = place(me_ref)
    for c, at, y in last_of(na, nc, u_ref, refs[:-1], spot):
        refs[-1][c, at, :] = y


def local(x):
    return pltpu.with_memory_space_constraint(x, pltpu.VMEM)


def call(kernel, outs, scalars, arrays, scratch=(), specs=None):
    return pl.pallas_call(
        kernel,
        out_shape=outs,
        in_specs=[SM] * len(scalars) + (specs or [VM] * len(arrays)),
        out_specs=[VM] * len(outs),
        scratch_shapes=list(scratch),
        compiler_params=pltpu.CompilerParams(vmem_limit_bytes=20 << 20),
        cost_estimate=pl.CostEstimate(flops=0, bytes_accessed=1 << 16, transcendentals=0),
    )(*scalars, *arrays)


def per_device(psi_prev, psi_cur, kin_stretch, kin_radius, potential, angular, pattern, quanta):
    nc, nr, nb = psi_cur.shape
    lam = potential.shape[0]
    nd = lax.axis_size("chan")
    n = nd // TEAM
    na = nr // n
    total_ch = nc * nd
    cb = total_ch // pattern.shape[1]
    me = lax.axis_index("chan").astype(jnp.int32).reshape(1)
    sds = jax.ShapeDtypeStruct

    def swap(x, bits):
        return lax.ppermute(x, "chan", [(i, i ^ bits) for i in range(nd)])

    def across(x, bits):
        return local(swap(x, bits))

    def exchange(pieces):
        return [across(x, hop(i, n) * TEAM) if i else x for i, x in enumerate(pieces)]

    def after(x, *others):
        return lax.optimization_barrier((x, *others))[0]

    def gather(x, beside):
        over = local(after(swap(x, 2), *beside))
        return [[y] for y in (x, across(x, 1), over, across(over, 1))]

    def gather_near_far(near, far, *beside):
        over = local(after(swap(near, 2), *beside))
        rows = [[x, across(x, 1), y, across(y, 1)] for x, y in ((far, across(far, 2)), (near, over))]
        return list(zip(*rows))

    piece = pltpu.VMEM((na * nc, nb), F32)
    packed = pltpu.VMEM((n, na * nc, nb), F32)
    square = pltpu.VMEM((8, nb), F32)
    on_chip = pltpu.VMEM((nc, nr, nb), F32)
    natural = sds((nc, nr, nb), F32)
    split = pltpu.VMEM((nd, nc, max(1, na // 2) * nb), BF16)

    def kinetic(prev, cur=(), pieces=(), base=(), n_out=0, out=()):
        kernel = functools.partial(kinetic_kernel, na, nc, n, len(pieces), len(base), n_out)
        arrays = [kin_stretch, kin_radius, prev, *pieces, *base, *cur]
        return call(kernel, [piece] * n_out + [on_chip, *out], [me, quanta], arrays)

    def mix(sources):
        arrays = [coup, potential, *(x for source in sources for x in source)]
        return call(functools.partial(mix_kernel, nc, n, len(sources[0])), [piece] * n, [me], arrays, [split, split])

    def join(terms, where=None, split_too=False, behind=()):
        size = len(terms[0])
        n_out = size if split_too else 0
        outs = [pltpu.VMEM((size, na * nc, nb), F32)] + [piece] * n_out + [square] * (len(terms) > 1)
        specs = [VM] * (size * len(terms)) + [ANY] * len(behind)
        kernel = functools.partial(join_kernel, where or [None] * size, len(terms), n_out, len(behind))
        return call(kernel, outs, [me], [x for t in terms for x in t] + list(behind), (), specs)

    (coup,) = call(
        functools.partial(coupling_kernel, cb, nc, n),
        [pltpu.VMEM((lam, 2, n, nc, total_ch), BF16)],
        [me, pattern],
        [angular],
        [pltpu.VMEM((lam, n, nc, total_ch), F32), pltpu.SemaphoreType.DMA((lam * n,))],
        [pl.BlockSpec(memory_space=pltpu.HBM)],
    )
    v1 = exchange(call(functools.partial(to_pieces_kernel, na, nc), [piece] * n, [me], [psi_cur]))
    *u1, u1_nat = kinetic(psi_prev, [psi_cur], n_out=n)
    near, far = ([*join([part])][0] for part in near_far(v1))
    w1 = mix(gather_near_far(near, far, coup, u1_nat))
    u1 = exchange(u1)
    v2, s2 = join([w1, u1], [hop(i, n) for i in range(n)])
    w1 = exchange(w1)
    *u2, _, v2_nat = kinetic(psi_cur, pieces=w1, base=[u1_nat], n_out=n, out=[on_chip])
    w2 = near_far(mix(gather(v2, w1[1:])))
    u2 = near_far(exchange(u2))
    near, *v3_near, s3 = join([w2[0], u2[0]], split_too=True)
    far, *v3_far, s3_far = join([w2[1], u2[1]], split_too=True, behind=[near])
    v3 = exchange([v3_near[0], *v3_far, v3_near[1]])
    u3, prev_out = kinetic(v2_nat, pieces=v3, out=[natural])
    w3 = exchange(mix(gather_near_far(near, far, v3[1])))
    (sums,) = call(functools.partial(norm_kernel, na, nc, n), [sds((8, nb), F32)], [me], [u3, *w3, s2, s3, s3_far])
    (cur_out,) = call(functools.partial(finish_kernel, na, nc), [natural], [me], [u3, *w3])
    bit = 1
    while bit < nd:
        sums = (sums + swap(sums, bit)) + (swap(sums, 2 * bit) + swap(sums, 3 * bit))
        bit *= 4
    norms = jnp.sum(sums[:ITERS], axis=1) / (total_ch * nr * nb)
    return prev_out, cur_out, norms


def solution(mesh):
    return jax.shard_map(
        per_device,
        mesh=mesh,
        in_specs=(
            P(("groups", "chan"), None, None),
            P(("groups", "chan"), None, None),
            P(),
            P(),
            P(),
            P("groups", None, None),
            P("groups", None),
            P(("groups", "chan"), None),
        ),
        out_specs=(
            P(("groups", "chan"), None, None),
            P(("groups", "chan"), None, None),
            P("groups"),
        ),
        check_vma=False,
    )
```

```python
import functools

import jax
import jax.numpy as jnp
import numpy as np
from jax import lax
from jax.experimental import pallas as pl
from jax.experimental.pallas import tpu as pltpu
from jax.sharding import PartitionSpec as P

JL_MAX = 40
ITERS = 3
TEAM = 4
F32 = jnp.float32
BF16 = jnp.bfloat16
HP = lax.Precision.HIGHEST
VM = pl.BlockSpec(memory_space=pltpu.VMEM)
SM = pl.BlockSpec(memory_space=pltpu.SMEM)
ANY = pl.BlockSpec(memory_space=pl.ANY)


def hop(i, n):
    return i % (n - 1) + 1 if i else 0


def place(me_ref):
    return me_ref[0] // TEAM, me_ref[0] % TEAM


def rows_of(spot, s, n, na):
    return pl.ds(pl.multiple_of((spot ^ hop(s, n)) * na, na), na)


def to_pieces_kernel(na, nc, me_ref, x_ref, *outs):
    spot, _ = place(me_ref)
    for s, out in enumerate(outs):
        for c in range(nc):
            out[pl.ds(c, na, stride=nc), :] = x_ref[c, rows_of(spot, s, len(outs), na), :]


def kinetic_kernel(na, nc, n, n_in, based, n_out, me_ref, quanta, ks, kr, prev, *refs):
    spot, _ = place(me_ref)
    refs = list(refs)
    take = lambda k: [refs.pop(0) for _ in range(k)]
    pieces = take(n_in)
    base = refs.pop(0) if based else None
    cur = None if n_in else refs.pop(0)
    u_refs = take(n_out)
    y_ref = refs.pop(0)
    cur = refs.pop(0) if n_in else cur
    nr, nb = prev.shape[1:]

    def placed(some):
        if len(some) == 1:
            return [(some[0].at[z], pl.ds(z * na, na)) for z in range(n)]
        return [(ref, rows_of(spot, s, n, na)) for s, ref in enumerate(some)]

    kstr = 2.0 * ks[...]
    krad = 2.0 * kr[...]
    stretch = 1.0 + lax.broadcasted_iota(jnp.int32, (nr, nb), 0).astype(F32) / nr
    radius = 1.0 + 3.0 * lax.broadcasted_iota(jnp.int32, (nr, nb), 1).astype(F32) / nb
    rotation = 1.0 / (stretch * stretch)
    orbital = 1.0 / (radius * radius)
    scale = np.float32(0.3 / (JL_MAX * (JL_MAX - 1)))
    group = min(8, nc)
    for start in range(0, nc, group):
        chans = range(start, start + group)
        for piece, at in placed(pieces):
            for c in chans:
                x = piece[pl.ds(c, na, stride=nc), :]
                cur[c, at, :] = x + base[c, at, :] if based else x
        tiles = [cur[c] for c in chans]
        mixed_a = jnp.dot(kstr, jnp.concatenate(tiles, 1), precision=HP, preferred_element_type=F32)
        mixed_b = jnp.dot(jnp.concatenate(tiles, 0), krad, precision=HP, preferred_element_type=F32)
        for i, c in enumerate(chans):
            j = quanta[0, c].astype(F32)
            l = quanta[1, c].astype(F32)
            barrier = orbital * (scale * (l * (l + 1.0))) + rotation * (scale * (j * (j + 1.0))) - 0.2
            y = mixed_a[:, i * nb : (i + 1) * nb] + mixed_b[i * nr : (i + 1) * nr]
            y_ref[c] = y + barrier * tiles[i] - prev[c]
        for u, at in placed(u_refs):
            for c in chans:
                u[pl.ds(c, na, stride=nc), :] = y_ref[c, at, :]


def coupling_kernel(cb, nc, n, me_ref, pat_ref, ang_ref, out_ref, buf, sems):
    spot, seat = place(me_ref)
    lam, _, tot = ang_ref.shape

    def row(s):
        return ((spot ^ hop(s, n)) * TEAM + seat) * nc

    copies = [
        pltpu.make_async_copy(
            ang_ref.at[m, pl.ds(pl.multiple_of(row(z), nc), nc), :], buf.at[m, z], sems.at[m * n + z]
        )
        for m in range(lam)
        for z in range(n)
    ]
    for copy in copies:
        copy.start()
    lane = lax.broadcasted_iota(jnp.int32, (nc, tot), 1) // cb
    for copy in copies:
        copy.wait()
    for z in range(n):
        factor = jnp.zeros((nc, tot), F32)
        for k in range(tot // cb):
            factor = jnp.where(lane == k, pat_ref[row(z) // cb, k].astype(F32), factor)
        for m in range(lam):
            val = buf[m, z] * factor
            hi = val.astype(BF16)
            out_ref[m, 0, z] = hi
            out_ref[m, 1, z] = (val - hi.astype(F32)).astype(BF16)


def mix_kernel(nc, n, n_ref, me_ref, coup, pot, *refs):
    spot, seat = place(me_ref)
    sources, pieces = refs[: TEAM * n_ref], refs[TEAM * n_ref : -2]
    xs_hi, xs_lo = refs[-2:]
    rows, nb = pieces[0].shape
    na, ch = rows // nc, n * nc
    lam, tot = coup.shape[0], coup.shape[-1]
    step = max(1, na // 2)
    for k0 in range(0, na, step):
        ks = range(k0, k0 + step)
        for m in range(TEAM):
            for s in range(n):
                if n_ref == 1:
                    z, src = s, sources[m].at[s]
                else:
                    far = s % (n - 1) > 0
                    z, src = spot ^ hop(s, n), sources[m * 2 + (not far)].at[s - 1 if far else s // (n - 1)]
                x = jnp.concatenate([src[k * nc : (k + 1) * nc] for k in ks], 1)
                hi = x.astype(BF16)
                xs_hi[z * TEAM + (seat ^ m)] = hi
                xs_lo[z * TEAM + (seat ^ m)] = (x - hi.astype(F32)).astype(BF16)
        x_hi = xs_hi[...].reshape(tot, step * nb)
        x_lo = xs_lo[...].reshape(tot, step * nb)
        acc = None
        for m in range(lam):
            both = coup[m].reshape(2 * ch, tot)
            p = jnp.dot(both, x_hi, preferred_element_type=F32)
            p = p[:ch] + p[ch:] + jnp.dot(both[:ch], x_lo, preferred_element_type=F32)
            w = jnp.concatenate([pot[m, pl.ds(spot * na + k, 1), :] for k in ks], 1)
            p = p * (2.0 * w)
            acc = p if acc is None else acc + p
        for s, piece in enumerate(pieces):
            for i, k in enumerate(ks):
                piece[k * nc : (k + 1) * nc] = acc[s * nc : (s + 1) * nc, i * nb : (i + 1) * nb]


def near_far(pieces):
    return [pieces[0], pieces[-1]], pieces[1:-1]


def group_kernel(n, me_ref, *refs):
    for s in range(n):
        refs[-1][s] = refs[s][...]


def join_kernel(n, me_ref, u_ref, *refs):
    spot, _ = place(me_ref)
    out, sq = refs[-2:]
    total = 0.0
    for s in range(n):
        at = spot ^ hop(s, n)
        y = refs[s][...] + u_ref[at]
        out[at] = y
        total = total + jnp.sum((y * y).reshape(-1, 8, y.shape[1]), axis=0)
    sq[...] = total


def group_join_kernel(n, n_all, me_ref, *refs):
    spot, _ = place(me_ref)
    ws, us, rest = refs[:n], refs[n : 2 * n], refs[2 * n :]
    near, out, sq = rest[0] if n_all else None, rest[-2 - bool(n_all)], rest[-1 - bool(n_all)]
    total = 0.0
    for s in range(n):
        y = ws[s][...] + us[s][...]
        out[s] = y
        if n_all:
            rest[-1][spot ^ hop(s + 1, n_all)] = y
        total = total + jnp.sum((y * y).reshape(-1, 8, y.shape[1]), axis=0)
    if n_all:
        rest[-1][spot] = near[0]
        rest[-1][spot ^ hop(n_all - 1, n_all)] = near[1]
    sq[...] = total


def last_of(na, nc, u_ref, pieces, spot):
    for s, piece in enumerate(pieces):
        at = rows_of(spot, s, len(pieces), na)
        for c in range(nc):
            yield c, at, u_ref[c, at, :] + piece[pl.ds(c, na, stride=nc), :]


def norm_kernel(na, nc, n, me_ref, u_ref, *refs):
    spot, _ = place(me_ref)
    nb = u_ref.shape[-1]
    total = jnp.zeros((na, nb), F32)
    for _, _, y in last_of(na, nc, u_ref, refs[:n], spot):
        total = total + y * y
    squares = [r[...] for r in refs[n:-1]]
    tiles = [jnp.sum(t, axis=0, keepdims=True) for t in (squares[0], sum(squares[2:], squares[1]), total)]
    refs[-1][...] = jnp.concatenate([*tiles, jnp.zeros((8 - ITERS, nb), F32)], 0)


def finish_kernel(na, nc, me_ref, u_ref, *refs):
    spot, _ = place(me_ref)
    for c, at, y in last_of(na, nc, u_ref, refs[:-1], spot):
        refs[-1][c, at, :] = y


def local(x):
    return pltpu.with_memory_space_constraint(x, pltpu.VMEM)


def call(kernel, outs, scalars, arrays, scratch=(), specs=None):
    return pl.pallas_call(
        kernel,
        out_shape=outs,
        in_specs=[SM] * len(scalars) + (specs or [VM] * len(arrays)),
        out_specs=[VM] * len(outs),
        scratch_shapes=list(scratch),
        compiler_params=pltpu.CompilerParams(vmem_limit_bytes=20 << 20),
        cost_estimate=pl.CostEstimate(flops=0, bytes_accessed=1 << 16, transcendentals=0),
    )(*scalars, *arrays)


def per_device(psi_prev, psi_cur, kin_stretch, kin_radius, potential, angular, pattern, quanta):
    nc, nr, nb = psi_cur.shape
    lam = potential.shape[0]
    nd = lax.axis_size("chan")
    n = nd // TEAM
    na = nr // n
    total_ch = nc * nd
    cb = total_ch // pattern.shape[1]
    me = lax.axis_index("chan").astype(jnp.int32).reshape(1)
    sds = jax.ShapeDtypeStruct

    def swap(x, bits):
        return lax.ppermute(x, "chan", [(i, i ^ bits) for i in range(nd)])

    def across(x, bits):
        return local(swap(x, bits))

    def exchange(pieces):
        return [across(x, hop(i, n) * TEAM) if i else x for i, x in enumerate(pieces)]

    def exchange_all(x):
        lines = [[spot * TEAM + seat for spot in range(n)] for seat in range(TEAM)]
        return local(lax.all_to_all(x, "chan", 0, 0, tiled=True, axis_index_groups=lines))

    def after(x, *others):
        return lax.optimization_barrier((x, *others))[0]

    def gather(x, beside):
        over = local(after(swap(x, 2), *beside))
        return [[y] for y in (x, across(x, 1), over, across(over, 1))]

    def gather_near_far(near, far, *beside):
        over = local(after(swap(near, 2), *beside))
        rows = [[x, across(x, 1), y, across(y, 1)] for x, y in ((far, across(far, 2)), (near, over))]
        return list(zip(*rows))

    piece = pltpu.VMEM((na * nc, nb), F32)
    packed = pltpu.VMEM((n, na * nc, nb), F32)
    square = pltpu.VMEM((8, nb), F32)
    on_chip = pltpu.VMEM((nc, nr, nb), F32)
    natural = sds((nc, nr, nb), F32)
    split = pltpu.VMEM((nd, nc, max(1, na // 2) * nb), BF16)

    def kinetic(prev, cur=(), pieces=(), base=(), n_out=0, out=()):
        kernel = functools.partial(kinetic_kernel, na, nc, n, len(pieces), len(base), n_out)
        arrays = [kin_stretch, kin_radius, prev, *pieces, *base, *cur]
        outs = [packed] if n_out == 1 else [piece] * n_out
        return call(kernel, [*outs, on_chip, *out], [me, quanta.T], arrays)

    def mix(sources):
        arrays = [coup, potential, *(x for source in sources for x in source)]
        return call(functools.partial(mix_kernel, nc, n, len(sources[0])), [piece] * n, [me], arrays, [split, split])

    def group(pieces, behind=()):
        k = len(pieces)
        specs = [VM] * k + [ANY] * len(behind)
        kernel = functools.partial(group_kernel, k)
        return call(kernel, [pltpu.VMEM((k, na * nc, nb), F32)], [me], [*pieces, *behind], (), specs)[0]

    def group_join(ws, us, near=()):
        k = len(ws)
        kernel = functools.partial(group_join_kernel, k, n if near else 0)
        outs = [pltpu.VMEM((k, na * nc, nb), F32), square] + [packed] * len(near)
        return call(kernel, outs, [me], [*ws, *us, *near])

    (coup,) = call(
        functools.partial(coupling_kernel, cb, nc, n),
        [pltpu.VMEM((lam, 2, n, nc, total_ch), BF16)],
        [me, pattern],
        [pltpu.with_memory_space_constraint(angular, pltpu.HBM)],
        [pltpu.VMEM((lam, n, nc, total_ch), F32), pltpu.SemaphoreType.DMA((lam * n,))],
        [pl.BlockSpec(memory_space=pltpu.HBM)],
    )
    v1 = exchange(call(functools.partial(to_pieces_kernel, na, nc), [piece] * n, [me], [psi_cur]))
    u1, u1_nat = kinetic(psi_prev, [psi_cur], n_out=1)
    u1 = exchange_all(u1)
    near, far = near_far(v1)
    w1 = mix(gather_near_far(group(near, [u1_nat]), group(far), coup))
    w1_c = exchange(w1)
    v2, s2 = call(functools.partial(join_kernel, n), [packed, square], [me], [u1, *w1])
    *u2, _, v2_nat = kinetic(psi_cur, pieces=w1_c, base=[u1_nat], n_out=n, out=[on_chip])
    w2 = near_far(mix(gather(v2, w1_c[1:])))
    u2 = near_far(exchange(u2))
    near, s3 = group_join(w2[0], u2[0])
    far, s3_far, v3 = group_join(w2[1], u2[1], [near])
    v3 = exchange_all(v3)
    u3, prev_out = kinetic(v2_nat, pieces=[v3], out=[natural])
    w3 = exchange(mix(gather_near_far(near, far)))
    (sums,) = call(functools.partial(norm_kernel, na, nc, n), [sds((8, nb), F32)], [me], [u3, *w3, s2, s3, s3_far])
    (cur_out,) = call(functools.partial(finish_kernel, na, nc), [natural], [me], [u3, *w3])
    bit = 1
    while bit < nd:
        sums = (sums + swap(sums, bit)) + (swap(sums, 2 * bit) + swap(sums, 3 * bit))
        bit *= 4
    norms = jnp.sum(sums[:ITERS], axis=1) / (total_ch * nr * nb)
    return prev_out, cur_out, norms


def solution(mesh):
    return jax.shard_map(
        per_device,
        mesh=mesh,
        in_specs=(
            P(("groups", "chan"), None, None),
            P(("groups", "chan"), None, None),
            P(),
            P(),
            P(),
            P("groups", None, None),
            P("groups", None),
            P(("groups", "chan"), None),
        ),
        out_specs=(
            P(("groups", "chan"), None, None),
            P(("groups", "chan"), None, None),
            P("groups"),
        ),
        check_vma=False,
    )
```

```python
import functools

import jax
import jax.numpy as jnp
import numpy as np
from jax import lax
from jax.experimental import pallas as pl
from jax.experimental.pallas import tpu as pltpu
from jax.sharding import PartitionSpec as P

JL_MAX = 40
ITERS = 3
TEAM = 4
F32 = jnp.float32
BF16 = jnp.bfloat16
HP = lax.Precision.HIGHEST
VM = pl.BlockSpec(memory_space=pltpu.VMEM)
SM = pl.BlockSpec(memory_space=pltpu.SMEM)
ANY = pl.BlockSpec(memory_space=pl.ANY)


def hop(i, n):
    return i % (n - 1) + 1 if i else 0


def place(me_ref):
    return me_ref[0] // TEAM, me_ref[0] % TEAM


def rows_of(spot, s, n, na):
    return pl.ds(pl.multiple_of((spot ^ hop(s, n)) * na, na), na)


def to_pieces_kernel(na, nc, me_ref, x_ref, *outs):
    spot, _ = place(me_ref)
    for s, out in enumerate(outs):
        for c in range(nc):
            out[pl.ds(c, na, stride=nc), :] = x_ref[c, rows_of(spot, s, len(outs), na), :]


def kinetic_kernel(na, nc, n, n_in, based, n_out, n_behind, me_ref, quanta, ks, kr, prev, *refs):
    spot, _ = place(me_ref)
    refs = list(refs)
    take = lambda k: [refs.pop(0) for _ in range(k)]
    pieces = take(n_in)
    base = refs.pop(0) if based else None
    cur = None if n_in else refs.pop(0)
    take(n_behind)
    u_refs = take(n_out)
    y_ref = refs.pop(0)
    cur = refs.pop(0) if n_in else cur
    nr, nb = prev.shape[1:]

    def placed(some):
        if len(some) == 1:
            return [(some[0].at[z], pl.ds(z * na, na)) for z in range(n)]
        return [(ref, rows_of(spot, s, n, na)) for s, ref in enumerate(some)]

    kstr = 2.0 * ks[...]
    krad = 2.0 * kr[...]
    stretch = 1.0 + lax.broadcasted_iota(jnp.int32, (nr, nb), 0).astype(F32) / nr
    radius = 1.0 + 3.0 * lax.broadcasted_iota(jnp.int32, (nr, nb), 1).astype(F32) / nb
    rotation = 1.0 / (stretch * stretch)
    orbital = 1.0 / (radius * radius)
    scale = np.float32(0.3 / (JL_MAX * (JL_MAX - 1)))
    group = min(8, nc)
    for start in range(0, nc, group):
        chans = range(start, start + group)
        for piece, at in placed(pieces):
            for c in chans:
                x = piece[pl.ds(c, na, stride=nc), :]
                cur[c, at, :] = x + base[c, at, :] if based else x
        tiles = [cur[c] for c in chans]
        mixed_a = jnp.dot(kstr, jnp.concatenate(tiles, 1), precision=HP, preferred_element_type=F32)
        mixed_b = jnp.dot(jnp.concatenate(tiles, 0), krad, precision=HP, preferred_element_type=F32)
        for i, c in enumerate(chans):
            j = quanta[0, c].astype(F32)
            l = quanta[1, c].astype(F32)
            barrier = orbital * (scale * (l * (l + 1.0))) + rotation * (scale * (j * (j + 1.0))) - 0.2
            y = mixed_a[:, i * nb : (i + 1) * nb] + mixed_b[i * nr : (i + 1) * nr]
            y_ref[c] = y + barrier * tiles[i] - prev[c]
        for u, at in placed(u_refs):
            for c in chans:
                u[pl.ds(c, na, stride=nc), :] = y_ref[c, at, :]


def coupling_kernel(cb, nc, n, me_ref, pat_ref, ang_ref, out_ref, buf, sems):
    spot, seat = place(me_ref)
    lam, _, tot = ang_ref.shape

    def row(s):
        return ((spot ^ hop(s, n)) * TEAM + seat) * nc

    copies = [
        pltpu.make_async_copy(
            ang_ref.at[m, pl.ds(pl.multiple_of(row(z), nc), nc), :], buf.at[m, z], sems.at[m * n + z]
        )
        for m in range(lam)
        for z in range(n)
    ]
    for copy in copies:
        copy.start()
    lane = lax.broadcasted_iota(jnp.int32, (nc, tot), 1) // cb
    for copy in copies:
        copy.wait()
    for z in range(n):
        factor = jnp.zeros((nc, tot), F32)
        for k in range(tot // cb):
            factor = jnp.where(lane == k, pat_ref[row(z) // cb, k].astype(F32), factor)
        for m in range(lam):
            val = buf[m, z] * factor
            hi = val.astype(BF16)
            out_ref[m, 0, z] = hi
            out_ref[m, 1, z] = (val - hi.astype(F32)).astype(BF16)


def mix_kernel(nc, n, n_ref, me_ref, coup, pot, *refs):
    spot, seat = place(me_ref)
    sources, pieces = refs[: TEAM * n_ref], refs[TEAM * n_ref : -2]
    xs_hi, xs_lo = refs[-2:]
    rows, nb = pieces[0].shape
    na, ch = rows // nc, n * nc
    lam, tot = coup.shape[0], coup.shape[-1]
    step = max(1, na // 2)
    for k0 in range(0, na, step):
        ks = range(k0, k0 + step)
        for m in range(TEAM):
            for s in range(n):
                if n_ref == 1:
                    z, src = s, sources[m].at[s]
                else:
                    far = s % (n - 1) > 0
                    z, src = spot ^ hop(s, n), sources[m * 2 + (not far)].at[s - 1 if far else s // (n - 1)]
                x = jnp.concatenate([src[k * nc : (k + 1) * nc] for k in ks], 1)
                hi = x.astype(BF16)
                xs_hi[z * TEAM + (seat ^ m)] = hi
                xs_lo[z * TEAM + (seat ^ m)] = (x - hi.astype(F32)).astype(BF16)
        x_hi = xs_hi[...].reshape(tot, step * nb)
        x_lo = xs_lo[...].reshape(tot, step * nb)
        acc = None
        for m in range(lam):
            both = coup[m].reshape(2 * ch, tot)
            p = jnp.dot(both, x_hi, preferred_element_type=F32)
            p = p[:ch] + p[ch:] + jnp.dot(both[:ch], x_lo, preferred_element_type=F32)
            w = jnp.concatenate([pot[m, pl.ds(spot * na + k, 1), :] for k in ks], 1)
            p = p * (2.0 * w)
            acc = p if acc is None else acc + p
        for s, piece in enumerate(pieces):
            for i, k in enumerate(ks):
                piece[k * nc : (k + 1) * nc] = acc[s * nc : (s + 1) * nc, i * nb : (i + 1) * nb]


def near_far(pieces):
    return [pieces[0], pieces[-1]], pieces[1:-1]


def group_kernel(n, me_ref, *refs):
    for s in range(n):
        refs[-1][s] = refs[s][...]


def join_kernel(n, me_ref, u_ref, *refs):
    spot, _ = place(me_ref)
    out, sq = refs[-2:]
    total = 0.0
    for s in range(n):
        at = spot ^ hop(s, n)
        y = refs[s][...] + u_ref[at]
        out[at] = y
        total = total + jnp.sum((y * y).reshape(-1, 8, y.shape[1]), axis=0)
    sq[...] = total


def group_join_kernel(n, me_ref, *refs):
    ws, us, (out, sq) = refs[:n], refs[n : 2 * n], refs[-2:]
    total = 0.0
    for s in range(n):
        y = ws[s][...] + us[s][...]
        out[s] = y
        total = total + jnp.sum((y * y).reshape(-1, 8, y.shape[1]), axis=0)
    sq[...] = total


def ungroup_kernel(n, me_ref, near, far, behind_ref, out):
    spot, _ = place(me_ref)
    out[spot] = near[0]
    out[spot ^ hop(n - 1, n)] = near[1]
    for s in range(1, n - 1):
        out[spot ^ hop(s, n)] = far[s - 1]


def last_of(na, nc, u_ref, pieces, spot):
    for s, piece in enumerate(pieces):
        at = rows_of(spot, s, len(pieces), na)
        for c in range(nc):
            yield c, at, u_ref[c, at, :] + piece[pl.ds(c, na, stride=nc), :]


def norm_kernel(na, nc, n, me_ref, u_ref, *refs):
    spot, _ = place(me_ref)
    nb = u_ref.shape[-1]
    total = jnp.zeros((na, nb), F32)
    for _, _, y in last_of(na, nc, u_ref, refs[:n], spot):
        total = total + y * y
    squares = [r[...] for r in refs[n:-1]]
    tiles = [jnp.sum(t, axis=0, keepdims=True) for t in (squares[0], sum(squares[2:], squares[1]), total)]
    refs[-1][...] = jnp.concatenate([*tiles, jnp.zeros((8 - ITERS, nb), F32)], 0)


def finish_kernel(na, nc, me_ref, u_ref, *refs):
    spot, _ = place(me_ref)
    for c, at, y in last_of(na, nc, u_ref, refs[:-1], spot):
        refs[-1][c, at, :] = y


def local(x):
    return pltpu.with_memory_space_constraint(x, pltpu.VMEM)


def call(kernel, outs, scalars, arrays, scratch=(), specs=None, flops=0):
    return pl.pallas_call(
        kernel,
        out_shape=outs,
        in_specs=[SM] * len(scalars) + (specs or [VM] * len(arrays)),
        out_specs=[VM] * len(outs),
        scratch_shapes=list(scratch),
        compiler_params=pltpu.CompilerParams(vmem_limit_bytes=20 << 20),
        cost_estimate=pl.CostEstimate(flops=flops, bytes_accessed=1 << 16, transcendentals=0),
    )(*scalars, *arrays)


def per_device(psi_prev, psi_cur, kin_stretch, kin_radius, potential, angular, pattern, quanta):
    nc, nr, nb = psi_cur.shape
    lam = potential.shape[0]
    nd = lax.axis_size("chan")
    n = nd // TEAM
    na = nr // n
    total_ch = nc * nd
    cb = total_ch // pattern.shape[1]
    me = lax.axis_index("chan").astype(jnp.int32).reshape(1)
    sds = jax.ShapeDtypeStruct

    def swap(x, bits):
        return lax.ppermute(x, "chan", [(i, i ^ bits) for i in range(nd)])

    def across(x, bits):
        return local(swap(x, bits))

    def exchange(pieces):
        return [across(x, hop(i, n) * TEAM) if i else x for i, x in enumerate(pieces)]

    def exchange_all(x):
        lines = [[spot * TEAM + seat for spot in range(n)] for seat in range(TEAM)]
        return local(lax.all_to_all(x, "chan", 0, 0, tiled=True, axis_index_groups=lines))

    def after(x, *others):
        return lax.optimization_barrier((x, *others))[0]

    def gather(x, beside):
        over = local(after(swap(x, 2), *beside))
        return [[y] for y in (x, across(x, 1), over, across(over, 1))]

    def gather_near_far(near, far, near_core, far_core, over):
        rows = [[x, y, z, across(z, 1)] for x, y, z in ((far, far_core, across(far, 2)), (near, near_core, over))]
        return list(zip(*rows))

    piece = pltpu.VMEM((na * nc, nb), F32)
    packed = pltpu.VMEM((n, na * nc, nb), F32)
    square = pltpu.VMEM((8, nb), F32)
    on_chip = pltpu.VMEM((nc, nr, nb), F32)
    natural = sds((nc, nr, nb), F32)
    split = pltpu.VMEM((nd, nc, max(1, na // 2) * nb), BF16)

    def kinetic(prev, cur=(), pieces=(), base=(), n_out=0, out=(), behind=()):
        kernel = functools.partial(kinetic_kernel, na, nc, n, len(pieces), len(base), n_out, len(behind))
        arrays = [kin_stretch, kin_radius, prev, *pieces, *base, *cur]
        outs = [packed] if n_out == 1 else [piece] * n_out
        specs = [VM] * len(arrays) + [ANY] * len(behind)
        return call(kernel, [*outs, on_chip, *out], [me, quanta.T], arrays + list(behind), (), specs)

    def mix(sources, flops=0):
        arrays = [coup, potential, *(x for source in sources for x in source)]
        kernel = functools.partial(mix_kernel, nc, n, len(sources[0]))
        return call(kernel, [piece] * n, [me], arrays, [split, split], flops=flops)

    def group(pieces, behind=()):
        k = len(pieces)
        specs = [VM] * k + [ANY] * len(behind)
        kernel = functools.partial(group_kernel, k)
        return call(kernel, [pltpu.VMEM((k, na * nc, nb), F32)], [me], [*pieces, *behind], (), specs)[0]

    def group_join(ws, us, behind=()):
        k = len(ws)
        outs = [pltpu.VMEM((k, na * nc, nb), F32), square]
        specs = [VM] * (2 * k) + [ANY] * len(behind)
        return call(functools.partial(group_join_kernel, k), outs, [me], [*ws, *us, *behind], (), specs)

    (coup,) = call(
        functools.partial(coupling_kernel, cb, nc, n),
        [pltpu.VMEM((lam, 2, n, nc, total_ch), BF16)],
        [me, pattern],
        [pltpu.with_memory_space_constraint(angular, pltpu.HBM)],
        [pltpu.VMEM((lam, n, nc, total_ch), F32), pltpu.SemaphoreType.DMA((lam * n,))],
        [pl.BlockSpec(memory_space=pltpu.HBM)],
        flops=5000000000,
    )
    v1 = exchange(call(functools.partial(to_pieces_kernel, na, nc), [piece] * n, [me], [psi_cur]))
    near, far = near_far(v1)
    near = group(near)
    u1, u1_nat = kinetic(psi_prev, [psi_cur], n_out=1)
    u1 = exchange_all(u1)
    far = group(far, [u1_nat])
    w1 = mix(gather_near_far(near, far, across(near, 1), across(far, 1), local(after(swap(near, 2), coup))), 0)
    w1_c = exchange(w1)
    v2, s2 = call(functools.partial(join_kernel, n), [packed, square], [me], [u1, *w1])
    *u2, _, v2_nat = kinetic(psi_cur, pieces=w1_c, base=[u1_nat], n_out=n, out=[on_chip])
    w2 = near_far(mix(gather(v2, w1_c[1:])))
    u2 = near_far(exchange(u2))
    near, s3 = group_join(w2[0], u2[0])
    near_core, near_over = across(near, 1), across(near, 2)
    far, s3_far = group_join(w2[1], u2[1], [near])
    far_core = across(far, 1)
    (v3,) = call(functools.partial(ungroup_kernel, n), [packed], [me], [near, far, far_core], (), [VM, VM, ANY])
    v3 = exchange_all(v3)
    u3, prev_out = kinetic(v2_nat, pieces=[v3], out=[natural])
    w3 = exchange(mix(gather_near_far(near, far, near_core, far_core, near_over), 2500000000))
    (sums,) = call(functools.partial(norm_kernel, na, nc, n), [sds((8, nb), F32)], [me], [u3, *w3, s2, s3, s3_far])
    (cur_out,) = call(functools.partial(finish_kernel, na, nc), [natural], [me], [u3, *w3])
    bit = 1
    while bit < nd:
        sums = (sums + swap(sums, bit)) + (swap(sums, 2 * bit) + swap(sums, 3 * bit))
        bit *= 4
    norms = jnp.sum(sums[:ITERS], axis=1) / (total_ch * nr * nb)
    return prev_out, cur_out, norms


def solution(mesh):
    return jax.shard_map(
        per_device,
        mesh=mesh,
        in_specs=(
            P(("groups", "chan"), None, None),
            P(("groups", "chan"), None, None),
            P(),
            P(),
            P(),
            P("groups", None, None),
            P("groups", None),
            P(("groups", "chan"), None),
        ),
        out_specs=(
            P(("groups", "chan"), None, None),
            P(("groups", "chan"), None, None),
            P("groups"),
        ),
        check_vma=False,
    )
```

```python
import functools

import jax
import jax.numpy as jnp
import numpy as np
from jax import lax
from jax.experimental import pallas as pl
from jax.experimental.pallas import tpu as pltpu
from jax.sharding import PartitionSpec as P

JL_MAX = 40
ITERS = 3
TEAM = 4
F32 = jnp.float32
BF16 = jnp.bfloat16
HP = lax.Precision.HIGHEST
VM = pl.BlockSpec(memory_space=pltpu.VMEM)
SM = pl.BlockSpec(memory_space=pltpu.SMEM)
ANY = pl.BlockSpec(memory_space=pl.ANY)


def hop(i, n):
    return i % (n - 1) + 1 if i else 0


def place(me_ref):
    return me_ref[0] // TEAM, me_ref[0] % TEAM


def rows_of(spot, s, n, na):
    return pl.ds(pl.multiple_of((spot ^ hop(s, n)) * na, na), na)


def to_pieces_kernel(na, nc, me_ref, x_ref, *outs):
    spot, _ = place(me_ref)
    for s, out in enumerate(outs):
        for c in range(nc):
            out[pl.ds(c, na, stride=nc), :] = x_ref[c, rows_of(spot, s, len(outs), na), :]


def kinetic_kernel(na, nc, n, n_in, based, n_out, n_behind, me_ref, quanta, ks, kr, prev, *refs):
    spot, _ = place(me_ref)
    refs = list(refs)
    take = lambda k: [refs.pop(0) for _ in range(k)]
    pieces = take(n_in)
    base = refs.pop(0) if based else None
    cur = None if n_in else refs.pop(0)
    take(n_behind)
    u_refs = take(n_out)
    y_ref = refs.pop(0)
    cur = refs.pop(0) if n_in else cur
    nr, nb = prev.shape[1:]

    def placed(some):
        if len(some) == 1:
            return [(some[0].at[z], pl.ds(z * na, na)) for z in range(n)]
        return [(ref, rows_of(spot, s, n, na)) for s, ref in enumerate(some)]

    kstr = 2.0 * ks[...]
    krad = 2.0 * kr[...]
    stretch = 1.0 + lax.broadcasted_iota(jnp.int32, (nr, nb), 0).astype(F32) / nr
    radius = 1.0 + 3.0 * lax.broadcasted_iota(jnp.int32, (nr, nb), 1).astype(F32) / nb
    rotation = 1.0 / (stretch * stretch)
    orbital = 1.0 / (radius * radius)
    scale = np.float32(0.3 / (JL_MAX * (JL_MAX - 1)))
    group = min(8, nc)
    for start in range(0, nc, group):
        chans = range(start, start + group)
        for piece, at in placed(pieces):
            for c in chans:
                x = piece[pl.ds(c, na, stride=nc), :]
                cur[c, at, :] = x + base[c, at, :] if based else x
        tiles = [cur[c] for c in chans]
        mixed_a = jnp.dot(kstr, jnp.concatenate(tiles, 1), precision=HP, preferred_element_type=F32)
        mixed_b = jnp.dot(jnp.concatenate(tiles, 0), krad, precision=HP, preferred_element_type=F32)
        for i, c in enumerate(chans):
            j = quanta[0, c].astype(F32)
            l = quanta[1, c].astype(F32)
            barrier = orbital * (scale * (l * (l + 1.0))) + rotation * (scale * (j * (j + 1.0))) - 0.2
            y = mixed_a[:, i * nb : (i + 1) * nb] + mixed_b[i * nr : (i + 1) * nr]
            y_ref[c] = y + barrier * tiles[i] - prev[c]
        for u, at in placed(u_refs):
            for c in chans:
                u[pl.ds(c, na, stride=nc), :] = y_ref[c, at, :]


def coupling_kernel(cb, nc, n, me_ref, pat_ref, ang_ref, out_ref, buf, sems):
    spot, seat = place(me_ref)
    lam, _, tot = ang_ref.shape

    def row(s):
        return ((spot ^ hop(s, n)) * TEAM + seat) * nc

    copies = [
        pltpu.make_async_copy(
            ang_ref.at[m, pl.ds(pl.multiple_of(row(z), nc), nc), :], buf.at[m, z], sems.at[m * n + z]
        )
        for m in range(lam)
        for z in range(n)
    ]
    for copy in copies:
        copy.start()
    lane = lax.broadcasted_iota(jnp.int32, (nc, tot), 1) // cb
    for copy in copies:
        copy.wait()
    for z in range(n):
        factor = jnp.zeros((nc, tot), F32)
        for k in range(tot // cb):
            factor = jnp.where(lane == k, pat_ref[row(z) // cb, k].astype(F32), factor)
        for m in range(lam):
            val = buf[m, z] * factor
            hi = val.astype(BF16)
            out_ref[m, 0, z] = hi
            out_ref[m, 1, z] = (val - hi.astype(F32)).astype(BF16)


def mix_kernel(nc, n, n_ref, me_ref, coup, pot, *refs):
    spot, seat = place(me_ref)
    sources, pieces = refs[: TEAM * n_ref], refs[TEAM * n_ref : -2]
    xs_hi, xs_lo = refs[-2:]
    rows, nb = pieces[0].shape
    na, ch = rows // nc, n * nc
    lam, tot = coup.shape[0], coup.shape[-1]
    step = max(1, na // 2)
    for k0 in range(0, na, step):
        ks = range(k0, k0 + step)
        for m in range(TEAM):
            for s in range(n):
                if n_ref == 1:
                    z, src = s, sources[m].at[s]
                else:
                    far = s % (n - 1) > 0
                    z, src = spot ^ hop(s, n), sources[m * 2 + (not far)].at[s - 1 if far else s // (n - 1)]
                x = jnp.concatenate([src[k * nc : (k + 1) * nc] for k in ks], 1)
                hi = x.astype(BF16)
                xs_hi[z * TEAM + (seat ^ m)] = hi
                xs_lo[z * TEAM + (seat ^ m)] = (x - hi.astype(F32)).astype(BF16)
        x_hi = xs_hi[...].reshape(tot, step * nb)
        x_lo = xs_lo[...].reshape(tot, step * nb)
        acc = None
        for m in range(lam):
            both = coup[m].reshape(2 * ch, tot)
            p = jnp.dot(both, x_hi, preferred_element_type=F32)
            p = p[:ch] + p[ch:] + jnp.dot(both[:ch], x_lo, preferred_element_type=F32)
            w = jnp.concatenate([pot[m, pl.ds(spot * na + k, 1), :] for k in ks], 1)
            p = p * (2.0 * w)
            acc = p if acc is None else acc + p
        for s, piece in enumerate(pieces):
            for i, k in enumerate(ks):
                piece[k * nc : (k + 1) * nc] = acc[s * nc : (s + 1) * nc, i * nb : (i + 1) * nb]


def near_far(pieces):
    return [pieces[0], pieces[-1]], pieces[1:-1]


def group_kernel(n, me_ref, *refs):
    for s in range(n):
        refs[-1][s] = refs[s][...]


def join_kernel(n, me_ref, u_ref, *refs):
    spot, _ = place(me_ref)
    out, sq = refs[-2:]
    total = 0.0
    for s in range(n):
        at = spot ^ hop(s, n)
        y = refs[s][...] + u_ref[at]
        out[at] = y
        total = total + jnp.sum((y * y).reshape(-1, 8, y.shape[1]), axis=0)
    sq[...] = total


def group_join_kernel(n, me_ref, *refs):
    ws, us, (out, sq) = refs[:n], refs[n : 2 * n], refs[-2:]
    total = 0.0
    for s in range(n):
        y = ws[s][...] + us[s][...]
        out[s] = y
        total = total + jnp.sum((y * y).reshape(-1, 8, y.shape[1]), axis=0)
    sq[...] = total


def ungroup_kernel(n, me_ref, near, far, behind_ref, out):
    spot, _ = place(me_ref)
    out[spot] = near[0]
    out[spot ^ hop(n - 1, n)] = near[1]
    for s in range(1, n - 1):
        out[spot ^ hop(s, n)] = far[s - 1]


def last_of(na, nc, u_ref, pieces, spot):
    for s, piece in enumerate(pieces):
        at = rows_of(spot, s, len(pieces), na)
        for c in range(nc):
            yield c, at, u_ref[c, at, :] + piece[pl.ds(c, na, stride=nc), :]


def norm_kernel(na, nc, n, me_ref, u_ref, *refs):
    spot, _ = place(me_ref)
    nb = u_ref.shape[-1]
    total = jnp.zeros((na, nb), F32)
    for _, _, y in last_of(na, nc, u_ref, refs[:n], spot):
        total = total + y * y
    squares = [r[...] for r in refs[n:-1]]
    tiles = [jnp.sum(t, axis=0, keepdims=True) for t in (squares[0], sum(squares[2:], squares[1]), total)]
    refs[-1][...] = jnp.concatenate([*tiles, jnp.zeros((8 - ITERS, nb), F32)], 0)


def finish_kernel(na, nc, me_ref, u_ref, *refs):
    spot, _ = place(me_ref)
    for c, at, y in last_of(na, nc, u_ref, refs[:-1], spot):
        refs[-1][c, at, :] = y


def local(x):
    return pltpu.with_memory_space_constraint(x, pltpu.VMEM)


def call(kernel, outs, scalars, arrays, scratch=(), specs=None, flops=0):
    return pl.pallas_call(
        kernel,
        out_shape=outs,
        in_specs=[SM] * len(scalars) + (specs or [VM] * len(arrays)),
        out_specs=[VM] * len(outs),
        scratch_shapes=list(scratch),
        compiler_params=pltpu.CompilerParams(vmem_limit_bytes=20 << 20),
        cost_estimate=pl.CostEstimate(flops=flops, bytes_accessed=1 << 16, transcendentals=0),
    )(*scalars, *arrays)


def per_device(psi_prev, psi_cur, kin_stretch, kin_radius, potential, angular, pattern, quanta):
    nc, nr, nb = psi_cur.shape
    lam = potential.shape[0]
    nd = lax.axis_size("chan")
    n = nd // TEAM
    na = nr // n
    total_ch = nc * nd
    cb = total_ch // pattern.shape[1]
    me = lax.axis_index("chan").astype(jnp.int32).reshape(1)
    sds = jax.ShapeDtypeStruct

    def swap(x, bits):
        return lax.ppermute(x, "chan", [(i, i ^ bits) for i in range(nd)])

    def across(x, bits):
        return local(swap(x, bits))

    def exchange(pieces):
        return [across(x, hop(i, n) * TEAM) if i else x for i, x in enumerate(pieces)]

    def exchange_all(x):
        lines = [[spot * TEAM + seat for spot in range(n)] for seat in range(TEAM)]
        return local(lax.all_to_all(x, "chan", 0, 0, tiled=True, axis_index_groups=lines))

    def after(x, *others):
        return lax.optimization_barrier((x, *others))[0]

    def gather(x, beside):
        over = local(after(swap(x, 2), *beside))
        return [[y] for y in (x, across(x, 1), over, across(over, 1))]

    def gather_near_far(near, far, near_core, far_core, over):
        rows = [[x, y, z, across(z, 1)] for x, y, z in ((far, far_core, across(far, 2)), (near, near_core, over))]
        return list(zip(*rows))

    piece = pltpu.VMEM((na * nc, nb), F32)
    packed = pltpu.VMEM((n, na * nc, nb), F32)
    square = pltpu.VMEM((8, nb), F32)
    on_chip = pltpu.VMEM((nc, nr, nb), F32)
    natural = sds((nc, nr, nb), F32)
    split = pltpu.VMEM((nd, nc, max(1, na // 2) * nb), BF16)

    def kinetic(prev, cur=(), pieces=(), base=(), n_out=0, out=(), behind=()):
        kernel = functools.partial(kinetic_kernel, na, nc, n, len(pieces), len(base), n_out, len(behind))
        arrays = [kin_stretch, kin_radius, prev, *pieces, *base, *cur]
        outs = [packed] if n_out == 1 else [piece] * n_out
        specs = [VM] * len(arrays) + [ANY] * len(behind)
        return call(kernel, [*outs, on_chip, *out], [me, quanta.T], arrays + list(behind), (), specs)

    def mix(sources, flops=0):
        arrays = [local(coup), local(potential), *(x for source in sources for x in source)]
        kernel = functools.partial(mix_kernel, nc, n, len(sources[0]))
        return call(kernel, [piece] * n, [me], arrays, [split, split], flops=flops)

    def group(pieces, behind=()):
        k = len(pieces)
        specs = [VM] * k + [ANY] * len(behind)
        kernel = functools.partial(group_kernel, k)
        return call(kernel, [pltpu.VMEM((k, na * nc, nb), F32)], [me], [*pieces, *behind], (), specs)[0]

    def group_join(ws, us, behind=()):
        k = len(ws)
        outs = [pltpu.VMEM((k, na * nc, nb), F32), square]
        specs = [VM] * (2 * k) + [ANY] * len(behind)
        return call(functools.partial(group_join_kernel, k), outs, [me], [*ws, *us, *behind], (), specs)

    (coup,) = call(
        functools.partial(coupling_kernel, cb, nc, n),
        [pltpu.VMEM((lam, 2, n, nc, total_ch), BF16)],
        [me, pattern],
        [pltpu.with_memory_space_constraint(angular, pltpu.HBM)],
        [pltpu.VMEM((lam, n, nc, total_ch), F32), pltpu.SemaphoreType.DMA((lam * n,))],
        [pl.BlockSpec(memory_space=pltpu.HBM)],
        flops=0,
    )
    v1 = exchange(call(functools.partial(to_pieces_kernel, na, nc), [piece] * n, [me], [psi_cur]))
    near, far = near_far(v1)
    near = group(near)
    near_core, near_over = across(near, 1), across(near, 2)
    u1, u1_nat = kinetic(psi_prev, [psi_cur], n_out=1)
    u1 = exchange_all(after(u1, near_over))
    far = group(far, [coup, u1_nat])
    w1 = mix(gather_near_far(near, far, near_core, across(far, 1), near_over), 5000000000)
    w1_c = exchange(w1)
    v2, s2 = call(functools.partial(join_kernel, n), [packed, square], [me], [u1, *w1])
    *u2, _, v2_nat = kinetic(psi_cur, pieces=w1_c, base=[u1_nat], n_out=n, out=[on_chip])
    w2 = near_far(mix(gather(v2, w1_c[1:]), 0))
    u2 = near_far(exchange(u2))
    near, s3 = group_join(w2[0], u2[0])
    near_core, near_over = across(near, 1), across(near, 2)
    far, s3_far = group_join(w2[1], u2[1], [near])
    far_core = across(far, 1)
    (v3,) = call(functools.partial(ungroup_kernel, n), [packed], [me], [near, far, far_core], (), [VM, VM, ANY])
    v3 = exchange_all(after(v3, near_over))
    u3, prev_out = kinetic(v2_nat, pieces=[v3], out=[natural])
    w3 = exchange(mix(gather_near_far(near, far, near_core, far_core, near_over), 2500000000))
    (sums,) = call(functools.partial(norm_kernel, na, nc, n), [sds((8, nb), F32)], [me], [u3, *w3, s2, s3, s3_far])
    (cur_out,) = call(functools.partial(finish_kernel, na, nc), [natural], [me], [u3, *w3])
    bit = 1
    while bit < nd:
        sums = (sums + swap(sums, bit)) + (swap(sums, 2 * bit) + swap(sums, 3 * bit))
        bit *= 4
    norms = jnp.sum(sums[:ITERS], axis=1) / (total_ch * nr * nb)
    return prev_out, cur_out, norms


def solution(mesh):
    return jax.shard_map(
        per_device,
        mesh=mesh,
        in_specs=(
            P(("groups", "chan"), None, None),
            P(("groups", "chan"), None, None),
            P(),
            P(),
            P(),
            P("groups", None, None),
            P("groups", None),
            P(("groups", "chan"), None),
        ),
        out_specs=(
            P(("groups", "chan"), None, None),
            P(("groups", "chan"), None, None),
            P("groups"),
        ),
        check_vma=False,
    )
```

```python
import functools

import jax
import jax.numpy as jnp
import numpy as np
from jax import lax
from jax.experimental import pallas as pl
from jax.experimental.pallas import tpu as pltpu
from jax.sharding import PartitionSpec as P

JL_MAX = 40
ITERS = 3
TEAM = 4
F32 = jnp.float32
BF16 = jnp.bfloat16
HP = lax.Precision.HIGHEST
VM = pl.BlockSpec(memory_space=pltpu.VMEM)
SM = pl.BlockSpec(memory_space=pltpu.SMEM)
ANY = pl.BlockSpec(memory_space=pl.ANY)


def hop(i, n):
    return i % (n - 1) + 1 if i else 0


def place(me_ref):
    return me_ref[0] // TEAM, me_ref[0] % TEAM


def rows_of(spot, s, n, na):
    return pl.ds(pl.multiple_of((spot ^ hop(s, n)) * na, na), na)


def to_pieces_kernel(na, nc, me_ref, x_ref, *outs):
    spot, _ = place(me_ref)
    for s, out in enumerate(outs):
        for c in range(nc):
            out[pl.ds(c, na, stride=nc), :] = x_ref[c, rows_of(spot, s, len(outs), na), :]


def kinetic_kernel(na, nc, n, n_in, based, n_out, n_behind, me_ref, quanta, ks, kr, prev, *refs):
    spot, _ = place(me_ref)
    refs = list(refs)
    take = lambda k: [refs.pop(0) for _ in range(k)]
    pieces = take(n_in)
    base = refs.pop(0) if based else None
    cur = None if n_in else refs.pop(0)
    take(n_behind)
    u_refs = take(n_out)
    y_ref = refs.pop(0)
    cur = refs.pop(0) if n_in else cur
    nr, nb = prev.shape[1:]

    def placed(some):
        if len(some) == 1:
            return [(some[0].at[z], pl.ds(z * na, na)) for z in range(n)]
        return [(ref, rows_of(spot, s, n, na)) for s, ref in enumerate(some)]

    kstr = 2.0 * ks[...]
    krad = 2.0 * kr[...]
    stretch = 1.0 + lax.broadcasted_iota(jnp.int32, (nr, nb), 0).astype(F32) / nr
    radius = 1.0 + 3.0 * lax.broadcasted_iota(jnp.int32, (nr, nb), 1).astype(F32) / nb
    rotation = 1.0 / (stretch * stretch)
    orbital = 1.0 / (radius * radius)
    scale = np.float32(0.3 / (JL_MAX * (JL_MAX - 1)))
    group = min(8, nc)
    for start in range(0, nc, group):
        chans = range(start, start + group)
        for piece, at in placed(pieces):
            for c in chans:
                x = piece[pl.ds(c, na, stride=nc), :]
                cur[c, at, :] = x + base[c, at, :] if based else x
        tiles = [cur[c] for c in chans]
        mixed_a = jnp.dot(kstr, jnp.concatenate(tiles, 1), precision=HP, preferred_element_type=F32)
        mixed_b = jnp.dot(jnp.concatenate(tiles, 0), krad, precision=HP, preferred_element_type=F32)
        for i, c in enumerate(chans):
            j = quanta[0, c].astype(F32)
            l = quanta[1, c].astype(F32)
            barrier = orbital * (scale * (l * (l + 1.0))) + rotation * (scale * (j * (j + 1.0))) - 0.2
            y = mixed_a[:, i * nb : (i + 1) * nb] + mixed_b[i * nr : (i + 1) * nr]
            y_ref[c] = y + barrier * tiles[i] - prev[c]
        for u, at in placed(u_refs):
            for c in chans:
                u[pl.ds(c, na, stride=nc), :] = y_ref[c, at, :]


def coupling_kernel(cb, nc, n, me_ref, pat_ref, ang_ref, out_ref, buf, sems):
    spot, seat = place(me_ref)
    lam, _, tot = ang_ref.shape

    def row(s):
        return ((spot ^ hop(s, n)) * TEAM + seat) * nc

    copies = [
        pltpu.make_async_copy(
            ang_ref.at[m, pl.ds(pl.multiple_of(row(z), nc), nc), :], buf.at[m, z], sems.at[m * n + z]
        )
        for m in range(lam)
        for z in range(n)
    ]
    for copy in copies:
        copy.start()
    lane = lax.broadcasted_iota(jnp.int32, (nc, tot), 1) // cb
    for copy in copies:
        copy.wait()
    for z in range(n):
        factor = jnp.zeros((nc, tot), F32)
        for k in range(tot // cb):
            factor = jnp.where(lane == k, pat_ref[row(z) // cb, k].astype(F32), factor)
        for m in range(lam):
            val = buf[m, z] * factor
            hi = val.astype(BF16)
            out_ref[m, 0, z] = hi
            out_ref[m, 1, z] = (val - hi.astype(F32)).astype(BF16)


def mix_kernel(nc, n, n_ref, me_ref, coup, pot, *refs):
    spot, seat = place(me_ref)
    sources, pieces = refs[: TEAM * n_ref], refs[TEAM * n_ref : -2]
    xs_hi, xs_lo = refs[-2:]
    rows, nb = pieces[0].shape
    na, ch = rows // nc, n * nc
    lam, tot = coup.shape[0], coup.shape[-1]
    step = max(1, na // 2)
    for k0 in range(0, na, step):
        ks = range(k0, k0 + step)
        for m in range(TEAM):
            for s in range(n):
                if n_ref == 1:
                    z, src = s, sources[m].at[s]
                else:
                    far = s % (n - 1) > 0
                    z, src = spot ^ hop(s, n), sources[m * 2 + (not far)].at[s - 1 if far else s // (n - 1)]
                x = jnp.concatenate([src[k * nc : (k + 1) * nc] for k in ks], 1)
                hi = x.astype(BF16)
                xs_hi[z * TEAM + (seat ^ m)] = hi
                xs_lo[z * TEAM + (seat ^ m)] = (x - hi.astype(F32)).astype(BF16)
        x_hi = xs_hi[...].reshape(tot, step * nb)
        x_lo = xs_lo[...].reshape(tot, step * nb)
        acc = None
        for m in range(lam):
            both = coup[m].reshape(2 * ch, tot)
            p = jnp.dot(both, x_hi, preferred_element_type=F32)
            p = p[:ch] + p[ch:] + jnp.dot(both[:ch], x_lo, preferred_element_type=F32)
            w = jnp.concatenate([pot[m, pl.ds(spot * na + k, 1), :] for k in ks], 1)
            p = p * (2.0 * w)
            acc = p if acc is None else acc + p
        for s, piece in enumerate(pieces):
            for i, k in enumerate(ks):
                piece[k * nc : (k + 1) * nc] = acc[s * nc : (s + 1) * nc, i * nb : (i + 1) * nb]


def near_far(pieces):
    return [pieces[0], pieces[-1]], pieces[1:-1]


def group_kernel(n, me_ref, *refs):
    for s in range(n):
        refs[-1][s] = refs[s][...]


def join_kernel(n, me_ref, u_ref, *refs):
    spot, _ = place(me_ref)
    out, sq = refs[-2:]
    total = 0.0
    for s in range(n):
        at = spot ^ hop(s, n)
        y = refs[s][...] + u_ref[at]
        out[at] = y
        total = total + jnp.sum((y * y).reshape(-1, 8, y.shape[1]), axis=0)
    sq[...] = total


def group_join_kernel(n, me_ref, *refs):
    ws, us, outs, (out, sq) = refs[:n], refs[n : 2 * n], refs[-2 - n : -2], refs[-2:]
    total = 0.0
    for s in range(n):
        y = ws[s][...] + us[s][...]
        out[s] = y
        outs[s][...] = y
        total = total + jnp.sum((y * y).reshape(-1, 8, y.shape[1]), axis=0)
    sq[...] = total


def last_of(na, nc, u_ref, pieces, spot):
    for s, piece in enumerate(pieces):
        at = rows_of(spot, s, len(pieces), na)
        for c in range(nc):
            yield c, at, u_ref[c, at, :] + piece[pl.ds(c, na, stride=nc), :]


def norm_kernel(na, nc, n, me_ref, u_ref, *refs):
    spot, _ = place(me_ref)
    nb = u_ref.shape[-1]
    total = jnp.zeros((na, nb), F32)
    for _, _, y in last_of(na, nc, u_ref, refs[:n], spot):
        total = total + y * y
    squares = [r[...] for r in refs[n:-1]]
    tiles = [jnp.sum(t, axis=0, keepdims=True) for t in (squares[0], sum(squares[2:], squares[1]), total)]
    refs[-1][...] = jnp.concatenate([*tiles, jnp.zeros((8 - ITERS, nb), F32)], 0)


def finish_kernel(na, nc, me_ref, u_ref, *refs):
    spot, _ = place(me_ref)
    for c, at, y in last_of(na, nc, u_ref, refs[:-1], spot):
        refs[-1][c, at, :] = y


def local(x):
    return pltpu.with_memory_space_constraint(x, pltpu.VMEM)


def call(kernel, outs, scalars, arrays, scratch=(), specs=None, flops=0):
    return pl.pallas_call(
        kernel,
        out_shape=outs,
        in_specs=[SM] * len(scalars) + (specs or [VM] * len(arrays)),
        out_specs=[VM] * len(outs),
        scratch_shapes=list(scratch),
        compiler_params=pltpu.CompilerParams(vmem_limit_bytes=20 << 20),
        cost_estimate=pl.CostEstimate(flops=flops, bytes_accessed=1 << 16, transcendentals=0),
    )(*scalars, *arrays)


def per_device(psi_prev, psi_cur, kin_stretch, kin_radius, potential, angular, pattern, quanta):
    nc, nr, nb = psi_cur.shape
    lam = potential.shape[0]
    nd = lax.axis_size("chan")
    n = nd // TEAM
    na = nr // n
    total_ch = nc * nd
    cb = total_ch // pattern.shape[1]
    me = lax.axis_index("chan").astype(jnp.int32).reshape(1)
    sds = jax.ShapeDtypeStruct

    def swap(x, bits):
        return lax.ppermute(x, "chan", [(i, i ^ bits) for i in range(nd)])

    def across(x, bits):
        return local(swap(x, bits))

    def exchange(pieces):
        return [across(x, hop(i, n) * TEAM) if i else x for i, x in enumerate(pieces)]

    def exchange_all(x):
        lines = [[spot * TEAM + seat for spot in range(n)] for seat in range(TEAM)]
        return local(lax.all_to_all(x, "chan", 0, 0, tiled=True, axis_index_groups=lines))

    def after(x, *others):
        return lax.optimization_barrier((x, *others))[0]

    def gather(x, beside):
        over = local(after(swap(x, 2), *beside))
        return [[y] for y in (x, across(x, 1), over, across(over, 1))]

    def gather_near_far(near, far, near_core, far_core, over):
        rows = [[x, y, z, across(z, 1)] for x, y, z in ((far, far_core, across(far, 2)), (near, near_core, over))]
        return list(zip(*rows))

    piece = pltpu.VMEM((na * nc, nb), F32)
    packed = pltpu.VMEM((n, na * nc, nb), F32)
    square = pltpu.VMEM((8, nb), F32)
    on_chip = pltpu.VMEM((nc, nr, nb), F32)
    natural = sds((nc, nr, nb), F32)
    split = pltpu.VMEM((nd, nc, max(1, na // 2) * nb), BF16)

    def kinetic(prev, cur=(), pieces=(), base=(), n_out=0, out=(), behind=()):
        kernel = functools.partial(kinetic_kernel, na, nc, n, len(pieces), len(base), n_out, len(behind))
        arrays = [kin_stretch, kin_radius, prev, *pieces, *base, *cur]
        outs = [packed] if n_out == 1 else [piece] * n_out
        specs = [VM] * len(arrays) + [ANY] * len(behind)
        return call(kernel, [*outs, on_chip, *out], [me, quanta.T], arrays + list(behind), (), specs)

    def mix(sources, flops=0):
        arrays = [local(coup), local(potential), *(x for source in sources for x in source)]
        kernel = functools.partial(mix_kernel, nc, n, len(sources[0]))
        return call(kernel, [piece] * n, [me], arrays, [split, split], flops=flops)

    def group(pieces, behind=()):
        k = len(pieces)
        specs = [VM] * k + [ANY] * len(behind)
        kernel = functools.partial(group_kernel, k)
        return call(kernel, [pltpu.VMEM((k, na * nc, nb), F32)], [me], [*pieces, *behind], (), specs)[0]

    def group_join(ws, us, behind=()):
        k = len(ws)
        outs = [piece] * k + [pltpu.VMEM((k, na * nc, nb), F32), square]
        specs = [VM] * (2 * k) + [ANY] * len(behind)
        return call(functools.partial(group_join_kernel, k), outs, [me], [*ws, *us, *behind], (), specs)

    (coup,) = call(
        functools.partial(coupling_kernel, cb, nc, n),
        [pltpu.VMEM((lam, 2, n, nc, total_ch), BF16)],
        [me, pattern],
        [pltpu.with_memory_space_constraint(angular, pltpu.HBM)],
        [pltpu.VMEM((lam, n, nc, total_ch), F32), pltpu.SemaphoreType.DMA((lam * n,))],
        [pl.BlockSpec(memory_space=pltpu.HBM)],
        flops=0,
    )
    v1 = exchange(call(functools.partial(to_pieces_kernel, na, nc), [piece] * n, [me], [psi_cur]))
    near, far = near_far(v1)
    near = group(near)
    near_core, near_over = across(near, 1), across(near, 2)
    u1, u1_nat = kinetic(psi_prev, [psi_cur], n_out=1)
    u1 = exchange_all(after(u1, near_over))
    far = group(far, [coup, u1_nat])
    w1 = mix(gather_near_far(near, far, near_core, across(far, 1), near_over), 5000000000)
    w1_c = exchange(w1)
    v2, s2 = call(functools.partial(join_kernel, n), [packed, square], [me], [u1, *w1])
    *u2, _, v2_nat = kinetic(psi_cur, pieces=w1_c, base=[u1_nat], n_out=n, out=[on_chip])
    w2 = near_far(mix(gather(v2, w1_c[1:]), 0))
    u2 = near_far(exchange(u2))
    *v3_near, near, s3 = group_join(w2[0], u2[0])
    *v3_far, far, s3_far = group_join(w2[1], u2[1], [near])
    v3 = exchange([v3_near[0], *v3_far, v3_near[1]])
    u3, prev_out = kinetic(v2_nat, pieces=v3, out=[natural])
    near_over = local(after(swap(near, 2), v3[1]))
    w3 = exchange(mix(gather_near_far(near, far, across(near, 1), across(far, 1), near_over), 0))
    (sums,) = call(functools.partial(norm_kernel, na, nc, n), [sds((8, nb), F32)], [me], [u3, *w3, s2, s3, s3_far])
    (cur_out,) = call(functools.partial(finish_kernel, na, nc), [natural], [me], [u3, *w3])
    bit = 1
    while bit < nd:
        sums = (sums + swap(sums, bit)) + (swap(sums, 2 * bit) + swap(sums, 3 * bit))
        bit *= 4
    norms = jnp.sum(sums[:ITERS], axis=1) / (total_ch * nr * nb)
    return prev_out, cur_out, norms


def solution(mesh):
    return jax.shard_map(
        per_device,
        mesh=mesh,
        in_specs=(
            P(("groups", "chan"), None, None),
            P(("groups", "chan"), None, None),
            P(),
            P(),
            P(),
            P("groups", None, None),
            P("groups", None),
            P(("groups", "chan"), None),
        ),
        out_specs=(
            P(("groups", "chan"), None, None),
            P(("groups", "chan"), None, None),
            P("groups"),
        ),
        check_vma=False,
    )
```

```python
import functools

import jax
import jax.numpy as jnp
import numpy as np
from jax import lax
from jax.experimental import pallas as pl
from jax.experimental.pallas import tpu as pltpu
from jax.sharding import PartitionSpec as P

JL_MAX = 40
ITERS = 3
TEAM = 4
F32 = jnp.float32
BF16 = jnp.bfloat16
HP = lax.Precision.HIGHEST
VM = pl.BlockSpec(memory_space=pltpu.VMEM)
SM = pl.BlockSpec(memory_space=pltpu.SMEM)
ANY = pl.BlockSpec(memory_space=pl.ANY)


def hop(i, n):
    return i % (n - 1) + 1 if i else 0


def place(me_ref):
    return me_ref[0] // TEAM, me_ref[0] % TEAM


def rows_of(spot, s, n, na):
    return pl.ds(pl.multiple_of((spot ^ hop(s, n)) * na, na), na)


def to_pieces_kernel(na, nc, me_ref, x_ref, *outs):
    spot, _ = place(me_ref)
    for s, out in enumerate(outs):
        for c in range(nc):
            out[pl.ds(c, na, stride=nc), :] = x_ref[c, rows_of(spot, s, len(outs), na), :]


def kinetic_kernel(na, nc, n, n_in, based, n_out, n_behind, me_ref, quanta, ks, kr, prev, *refs):
    spot, _ = place(me_ref)
    refs = list(refs)
    take = lambda k: [refs.pop(0) for _ in range(k)]
    pieces = take(n_in)
    base = refs.pop(0) if based else None
    cur = None if n_in else refs.pop(0)
    take(n_behind)
    u_refs = take(n_out)
    y_ref = refs.pop(0)
    cur = refs.pop(0) if n_in else cur
    nr, nb = prev.shape[1:]

    def placed(some):
        if len(some) == 1:
            return [(some[0].at[z], pl.ds(z * na, na)) for z in range(n)]
        return [(ref, rows_of(spot, s, n, na)) for s, ref in enumerate(some)]

    kstr = 2.0 * ks[...]
    krad = 2.0 * kr[...]
    stretch = 1.0 + lax.broadcasted_iota(jnp.int32, (nr, nb), 0).astype(F32) / nr
    radius = 1.0 + 3.0 * lax.broadcasted_iota(jnp.int32, (nr, nb), 1).astype(F32) / nb
    rotation = 1.0 / (stretch * stretch)
    orbital = 1.0 / (radius * radius)
    scale = np.float32(0.3 / (JL_MAX * (JL_MAX - 1)))
    group = min(8, nc)
    for start in range(0, nc, group):
        chans = range(start, start + group)
        for piece, at in placed(pieces):
            for c in chans:
                x = piece[pl.ds(c, na, stride=nc), :]
                cur[c, at, :] = x + base[c, at, :] if based else x
        tiles = [cur[c] for c in chans]
        mixed_a = jnp.dot(kstr, jnp.concatenate(tiles, 1), precision=HP, preferred_element_type=F32)
        mixed_b = jnp.dot(jnp.concatenate(tiles, 0), krad, precision=HP, preferred_element_type=F32)
        for i, c in enumerate(chans):
            j = quanta[0, c].astype(F32)
            l = quanta[1, c].astype(F32)
            barrier = orbital * (scale * (l * (l + 1.0))) + rotation * (scale * (j * (j + 1.0))) - 0.2
            y = mixed_a[:, i * nb : (i + 1) * nb] + mixed_b[i * nr : (i + 1) * nr]
            y_ref[c] = y + barrier * tiles[i] - prev[c]
        for u, at in placed(u_refs):
            for c in chans:
                u[pl.ds(c, na, stride=nc), :] = y_ref[c, at, :]


def coupling_kernel(cb, nc, n, me_ref, pat_ref, ang_ref, out_ref, buf, sems):
    spot, seat = place(me_ref)
    lam, _, tot = ang_ref.shape

    def row(s):
        return ((spot ^ hop(s, n)) * TEAM + seat) * nc

    copies = [
        pltpu.make_async_copy(
            ang_ref.at[m, pl.ds(pl.multiple_of(row(z), nc), nc), :], buf.at[m, z], sems.at[m * n + z]
        )
        for m in range(lam)
        for z in range(n)
    ]
    for copy in copies:
        copy.start()
    lane = lax.broadcasted_iota(jnp.int32, (nc, tot), 1) // cb
    for copy in copies:
        copy.wait()
    for z in range(n):
        factor = jnp.zeros((nc, tot), F32)
        for k in range(tot // cb):
            factor = jnp.where(lane == k, pat_ref[row(z) // cb, k].astype(F32), factor)
        for m in range(lam):
            val = buf[m, z] * factor
            hi = val.astype(BF16)
            out_ref[m, 0, z] = hi
            out_ref[m, 1, z] = (val - hi.astype(F32)).astype(BF16)


def mix_kernel(nc, n, n_ref, me_ref, coup, pot, *refs):
    spot, seat = place(me_ref)
    sources, pieces = refs[: TEAM * n_ref], refs[TEAM * n_ref : -2]
    xs_hi, xs_lo = refs[-2:]
    rows, nb = pieces[0].shape
    na, ch = rows // nc, n * nc
    lam, tot = coup.shape[0], coup.shape[-1]
    step = max(1, na // 2)
    for k0 in range(0, na, step):
        ks = range(k0, k0 + step)
        for m in range(TEAM):
            for s in range(n):
                if n_ref == 1:
                    z, src = s, sources[m].at[s]
                else:
                    far = s % (n - 1) > 0
                    z, src = spot ^ hop(s, n), sources[m * 2 + (not far)].at[s - 1 if far else s // (n - 1)]
                x = jnp.concatenate([src[k * nc : (k + 1) * nc] for k in ks], 1)
                hi = x.astype(BF16)
                xs_hi[z * TEAM + (seat ^ m)] = hi
                xs_lo[z * TEAM + (seat ^ m)] = (x - hi.astype(F32)).astype(BF16)
        x_hi = xs_hi[...].reshape(tot, step * nb)
        x_lo = xs_lo[...].reshape(tot, step * nb)
        acc = None
        for m in range(lam):
            both = coup[m].reshape(2 * ch, tot)
            p = jnp.dot(both, x_hi, preferred_element_type=F32)
            p = p[:ch] + p[ch:] + jnp.dot(both[:ch], x_lo, preferred_element_type=F32)
            w = jnp.concatenate([pot[m, pl.ds(spot * na + k, 1), :] for k in ks], 1)
            p = p * (2.0 * w)
            acc = p if acc is None else acc + p
        for s, piece in enumerate(pieces):
            for i, k in enumerate(ks):
                piece[k * nc : (k + 1) * nc] = acc[s * nc : (s + 1) * nc, i * nb : (i + 1) * nb]


def near_far(pieces):
    return [pieces[0], pieces[-1]], pieces[1:-1]


def group_kernel(n, me_ref, *refs):
    for s in range(n):
        refs[-1][s] = refs[s][...]


def held_kernel(me_ref, x_ref, behind_ref, out_ref):
    out_ref[...] = x_ref[...]


def join_kernel(n, me_ref, u_ref, *refs):
    spot, _ = place(me_ref)
    out, sq = refs[-2:]
    total = 0.0
    for s in range(n):
        at = spot ^ hop(s, n)
        y = refs[s][...] + u_ref[at]
        out[at] = y
        total = total + jnp.sum((y * y).reshape(-1, 8, y.shape[1]), axis=0)
    sq[...] = total


def group_join_kernel(n, me_ref, *refs):
    ws, us, outs, (out, sq) = refs[:n], refs[n : 2 * n], refs[-2 - n : -2], refs[-2:]
    total = 0.0
    for s in range(n):
        y = ws[s][...] + us[s][...]
        out[s] = y
        outs[s][...] = y
        total = total + jnp.sum((y * y).reshape(-1, 8, y.shape[1]), axis=0)
    sq[...] = total


def last_of(na, nc, u_ref, pieces, spot):
    for s, piece in enumerate(pieces):
        at = rows_of(spot, s, len(pieces), na)
        for c in range(nc):
            yield c, at, u_ref[c, at, :] + piece[pl.ds(c, na, stride=nc), :]


def norm_kernel(na, nc, n, me_ref, u_ref, *refs):
    spot, _ = place(me_ref)
    nb = u_ref.shape[-1]
    total = jnp.zeros((na, nb), F32)
    for _, _, y in last_of(na, nc, u_ref, refs[:n], spot):
        total = total + y * y
    squares = [r[...] for r in refs[n:-1]]
    tiles = [jnp.sum(t, axis=0, keepdims=True) for t in (squares[0], sum(squares[2:], squares[1]), total)]
    refs[-1][...] = jnp.concatenate([*tiles, jnp.zeros((8 - ITERS, nb), F32)], 0)


def finish_kernel(na, nc, me_ref, u_ref, *refs):
    spot, _ = place(me_ref)
    for c, at, y in last_of(na, nc, u_ref, refs[:-1], spot):
        refs[-1][c, at, :] = y


def local(x):
    return pltpu.with_memory_space_constraint(x, pltpu.VMEM)


def call(kernel, outs, scalars, arrays, scratch=(), specs=None, flops=0):
    return pl.pallas_call(
        kernel,
        out_shape=outs,
        in_specs=[SM] * len(scalars) + (specs or [VM] * len(arrays)),
        out_specs=[VM] * len(outs),
        scratch_shapes=list(scratch),
        compiler_params=pltpu.CompilerParams(vmem_limit_bytes=20 << 20),
        cost_estimate=pl.CostEstimate(flops=flops, bytes_accessed=1 << 16, transcendentals=0),
    )(*scalars, *arrays)


def per_device(psi_prev, psi_cur, kin_stretch, kin_radius, potential, angular, pattern, quanta):
    nc, nr, nb = psi_cur.shape
    lam = potential.shape[0]
    nd = lax.axis_size("chan")
    n = nd // TEAM
    na = nr // n
    total_ch = nc * nd
    cb = total_ch // pattern.shape[1]
    me = lax.axis_index("chan").astype(jnp.int32).reshape(1)
    sds = jax.ShapeDtypeStruct

    def swap(x, bits):
        return lax.ppermute(x, "chan", [(i, i ^ bits) for i in range(nd)])

    def across(x, bits):
        return local(swap(x, bits))

    def exchange(pieces):
        return [across(x, hop(i, n) * TEAM) if i else x for i, x in enumerate(pieces)]

    def exchange_all(x):
        lines = [[spot * TEAM + seat for spot in range(n)] for seat in range(TEAM)]
        return local(lax.all_to_all(x, "chan", 0, 0, tiled=True, axis_index_groups=lines))

    def after(x, *others):
        return lax.optimization_barrier((x, *others))[0]

    def gather(x, beside):
        over = local(after(swap(x, 2), *beside))
        return [[y] for y in (x, across(x, 1), over, across(over, 1))]

    def gather_near_far(near, far, near_core, far_core, over):
        rows = [[x, y, z, across(z, 1)] for x, y, z in ((far, far_core, across(far, 2)), (near, near_core, over))]
        return list(zip(*rows))

    piece = pltpu.VMEM((na * nc, nb), F32)
    packed = pltpu.VMEM((n, na * nc, nb), F32)
    square = pltpu.VMEM((8, nb), F32)
    on_chip = pltpu.VMEM((nc, nr, nb), F32)
    natural = sds((nc, nr, nb), F32)
    split = pltpu.VMEM((nd, nc, max(1, na // 2) * nb), BF16)

    def kinetic(prev, cur=(), pieces=(), base=(), n_out=0, out=(), behind=()):
        kernel = functools.partial(kinetic_kernel, na, nc, n, len(pieces), len(base), n_out, len(behind))
        arrays = [kin_stretch, kin_radius, prev, *pieces, *base, *cur]
        outs = [packed] if n_out == 1 else [piece] * n_out
        specs = [VM] * len(arrays) + [ANY] * len(behind)
        return call(kernel, [*outs, on_chip, *out], [me, quanta.T], arrays + list(behind), (), specs)

    def mix(sources, flops=0):
        arrays = [local(coup), local(potential), *(x for source in sources for x in source)]
        kernel = functools.partial(mix_kernel, nc, n, len(sources[0]))
        return call(kernel, [piece] * n, [me], arrays, [split, split], flops=flops)

    def group(pieces, behind=()):
        k = len(pieces)
        specs = [VM] * k + [ANY] * len(behind)
        kernel = functools.partial(group_kernel, k)
        return call(kernel, [pltpu.VMEM((k, na * nc, nb), F32)], [me], [*pieces, *behind], (), specs)[0]

    def group_join(ws, us, behind=()):
        k = len(ws)
        outs = [piece] * k + [pltpu.VMEM((k, na * nc, nb), F32), square]
        specs = [VM] * (2 * k) + [ANY] * len(behind)
        return call(functools.partial(group_join_kernel, k), outs, [me], [*ws, *us, *behind], (), specs)

    (coup,) = call(
        functools.partial(coupling_kernel, cb, nc, n),
        [pltpu.VMEM((lam, 2, n, nc, total_ch), BF16)],
        [me, pattern],
        [pltpu.with_memory_space_constraint(angular, pltpu.HBM)],
        [pltpu.VMEM((lam, n, nc, total_ch), F32), pltpu.SemaphoreType.DMA((lam * n,))],
        [pl.BlockSpec(memory_space=pltpu.HBM)],
        flops=0,
    )
    v1 = exchange(call(functools.partial(to_pieces_kernel, na, nc), [piece] * n, [me], [psi_cur]))
    near, far = near_far(v1)
    near = group(near)
    near_core, near_over = across(near, 1), across(near, 2)
    u1, u1_nat = kinetic(psi_prev, [psi_cur], n_out=1)
    u1 = exchange_all(call(held_kernel, [packed], [me], [u1, near_over], (), [VM, ANY])[0])
    far = group(far, [coup, u1_nat])
    w1 = mix(gather_near_far(near, far, near_core, across(far, 1), near_over), 5000000000)
    w1_c = exchange(w1)
    v2, s2 = call(functools.partial(join_kernel, n), [packed, square], [me], [u1, *w1])
    *u2, _, v2_nat = kinetic(psi_cur, pieces=w1_c, base=[u1_nat], n_out=n, out=[on_chip])
    w2 = near_far(mix(gather(v2, w1_c[1:]), 0))
    u2 = near_far(exchange(u2))
    *v3_near, near, s3 = group_join(w2[0], u2[0])
    *v3_far, far, s3_far = group_join(w2[1], u2[1], [near])
    v3 = exchange([v3_near[0], *v3_far, v3_near[1]])
    u3, prev_out = kinetic(v2_nat, pieces=v3, out=[natural])
    near_over = local(after(swap(near, 2), v3[1]))
    w3 = exchange(mix(gather_near_far(near, far, across(near, 1), across(far, 1), near_over), 0))
    (sums,) = call(functools.partial(norm_kernel, na, nc, n), [sds((8, nb), F32)], [me], [u3, *w3, s2, s3, s3_far])
    (cur_out,) = call(functools.partial(finish_kernel, na, nc), [natural], [me], [u3, *w3])
    bit = 1
    while bit < nd:
        sums = (sums + swap(sums, bit)) + (swap(sums, 2 * bit) + swap(sums, 3 * bit))
        bit *= 4
    norms = jnp.sum(sums[:ITERS], axis=1) / (total_ch * nr * nb)
    return prev_out, cur_out, norms


def solution(mesh):
    return jax.shard_map(
        per_device,
        mesh=mesh,
        in_specs=(
            P(("groups", "chan"), None, None),
            P(("groups", "chan"), None, None),
            P(),
            P(),
            P(),
            P("groups", None, None),
            P("groups", None),
            P(("groups", "chan"), None),
        ),
        out_specs=(
            P(("groups", "chan"), None, None),
            P(("groups", "chan"), None, None),
            P("groups"),
        ),
        check_vma=False,
    )
```

```python
import functools

import jax
import jax.numpy as jnp
import numpy as np
from jax import lax
from jax.experimental import pallas as pl
from jax.experimental.pallas import tpu as pltpu
from jax.sharding import PartitionSpec as P

JL_MAX = 40
ITERS = 3
TEAM = 4
F32 = jnp.float32
BF16 = jnp.bfloat16
VM = pl.BlockSpec(memory_space=pltpu.VMEM)
SM = pl.BlockSpec(memory_space=pltpu.SMEM)
ANY = pl.BlockSpec(memory_space=pl.ANY)


def hop(i, n):
    return i % (n - 1) + 1 if i else 0


def place(me_ref):
    return me_ref[0] // TEAM, me_ref[0] % TEAM


def rows_of(spot, s, n, na):
    return pl.ds(pl.multiple_of((spot ^ hop(s, n)) * na, na), na)


def halves(x):
    hi = x.astype(BF16)
    return hi, (x - hi.astype(F32)).astype(BF16)


def product(a, b):
    return sum(jnp.dot(a[i], b[j], preferred_element_type=F32) for i, j in ((0, 1), (1, 0), (0, 0)))


def to_pieces_kernel(na, nc, me_ref, x_ref, *outs):
    spot, _ = place(me_ref)
    for s, out in enumerate(outs):
        for c in range(nc):
            out[pl.ds(c, na, stride=nc), :] = x_ref[c, rows_of(spot, s, len(outs), na), :]


def kinetic_kernel(na, nc, n, n_in, based, n_out, n_behind, me_ref, quanta, ks, kr, prev, *refs):
    spot, _ = place(me_ref)
    refs = list(refs)
    take = lambda k: [refs.pop(0) for _ in range(k)]
    pieces = take(n_in)
    base = refs.pop(0) if based else None
    cur = None if n_in else refs.pop(0)
    take(n_behind)
    u_refs = take(n_out)
    y_ref = refs.pop(0)
    cur = refs.pop(0) if n_in else cur
    nr, nb = prev.shape[1:]

    def placed(some):
        if len(some) == 1:
            return [(some[0].at[z], pl.ds(z * na, na)) for z in range(n)]
        return [(ref, rows_of(spot, s, n, na)) for s, ref in enumerate(some)]

    kstr = halves(2.0 * ks[...])
    krad = halves(2.0 * kr[...])
    stretch = 1.0 + lax.broadcasted_iota(jnp.int32, (nr, nb), 0).astype(F32) / nr
    radius = 1.0 + 3.0 * lax.broadcasted_iota(jnp.int32, (nr, nb), 1).astype(F32) / nb
    rotation = 1.0 / (stretch * stretch)
    orbital = 1.0 / (radius * radius)
    scale = np.float32(0.3 / (JL_MAX * (JL_MAX - 1)))
    group = min(8, nc)
    for start in range(0, nc, group):
        chans = range(start, start + group)
        for piece, at in placed(pieces):
            for c in chans:
                x = piece[pl.ds(c, na, stride=nc), :]
                cur[c, at, :] = x + base[c, at, :] if based else x
        tiles = [cur[c] for c in chans]
        mixed_a = product(kstr, halves(jnp.concatenate(tiles, 1)))
        mixed_b = product(halves(jnp.concatenate(tiles, 0)), krad)
        for i, c in enumerate(chans):
            j = quanta[0, c].astype(F32)
            l = quanta[1, c].astype(F32)
            barrier = orbital * (scale * (l * (l + 1.0))) + rotation * (scale * (j * (j + 1.0))) - 0.2
            y = mixed_a[:, i * nb : (i + 1) * nb] + mixed_b[i * nr : (i + 1) * nr]
            y_ref[c] = y + barrier * tiles[i] - prev[c]
        for u, at in placed(u_refs):
            for c in chans:
                u[pl.ds(c, na, stride=nc), :] = y_ref[c, at, :]


def coupling_kernel(cb, nc, n, me_ref, pat_ref, ang_ref, out_ref, buf, sems):
    spot, seat = place(me_ref)
    lam, _, tot = ang_ref.shape

    def row(s):
        return ((spot ^ hop(s, n)) * TEAM + seat) * nc

    copies = [
        pltpu.make_async_copy(
            ang_ref.at[m, pl.ds(pl.multiple_of(row(z), nc), nc), :], buf.at[m, z], sems.at[m * n + z]
        )
        for m in range(lam)
        for z in range(n)
    ]
    for copy in copies:
        copy.start()
    lane = lax.broadcasted_iota(jnp.int32, (nc, tot), 1) // cb
    for copy in copies:
        copy.wait()
    for z in range(n):
        factor = jnp.zeros((nc, tot), F32)
        for k in range(tot // cb):
            factor = jnp.where(lane == k, pat_ref[row(z) // cb, k].astype(F32), factor)
        for m in range(lam):
            val = buf[m, z] * factor
            hi = val.astype(BF16)
            out_ref[m, 0, z] = hi
            out_ref[m, 1, z] = (val - hi.astype(F32)).astype(BF16)


def mix_kernel(nc, n, n_ref, me_ref, coup, pot, *refs):
    spot, seat = place(me_ref)
    sources, pieces = refs[: TEAM * n_ref], refs[TEAM * n_ref : -2]
    xs_hi, xs_lo = refs[-2:]
    rows, nb = pieces[0].shape
    na, ch = rows // nc, n * nc
    lam, tot = coup.shape[0], coup.shape[-1]
    step = max(1, na // 2)
    for k0 in range(0, na, step):
        ks = range(k0, k0 + step)
        for m in range(TEAM):
            for s in range(n):
                if n_ref == 1:
                    z, src = s, sources[m].at[s]
                else:
                    far = s % (n - 1) > 0
                    z, src = spot ^ hop(s, n), sources[m * 2 + (not far)].at[s - 1 if far else s // (n - 1)]
                x = jnp.concatenate([src[k * nc : (k + 1) * nc] for k in ks], 1)
                hi = x.astype(BF16)
                xs_hi[z * TEAM + (seat ^ m)] = hi
                xs_lo[z * TEAM + (seat ^ m)] = (x - hi.astype(F32)).astype(BF16)
        x_hi = xs_hi[...].reshape(tot, step * nb)
        x_lo = xs_lo[...].reshape(tot, step * nb)
        acc = None
        for m in range(lam):
            both = coup[m].reshape(2 * ch, tot)
            p = jnp.dot(both, x_hi, preferred_element_type=F32)
            p = p[:ch] + p[ch:] + jnp.dot(both[:ch], x_lo, preferred_element_type=F32)
            w = jnp.concatenate([pot[m, pl.ds(spot * na + k, 1), :] for k in ks], 1)
            p = p * (2.0 * w)
            acc = p if acc is None else acc + p
        for s, piece in enumerate(pieces):
            for i, k in enumerate(ks):
                piece[k * nc : (k + 1) * nc] = acc[s * nc : (s + 1) * nc, i * nb : (i + 1) * nb]


def near_far(pieces):
    return [pieces[0], pieces[-1]], pieces[1:-1]


def group_kernel(n, me_ref, *refs):
    for s in range(n):
        refs[-1][s] = refs[s][...]


def join_kernel(n, me_ref, u_ref, *refs):
    spot, _ = place(me_ref)
    out, sq = refs[-2:]
    total = 0.0
    for s in range(n):
        at = spot ^ hop(s, n)
        y = refs[s][...] + u_ref[at]
        out[at] = y
        total = total + jnp.sum((y * y).reshape(-1, 8, y.shape[1]), axis=0)
    sq[...] = total


def group_join_kernel(n, me_ref, *refs):
    ws, us, outs, (out, sq) = refs[:n], refs[n : 2 * n], refs[-2 - n : -2], refs[-2:]
    total = 0.0
    for s in range(n):
        y = ws[s][...] + us[s][...]
        out[s] = y
        outs[s][...] = y
        total = total + jnp.sum((y * y).reshape(-1, 8, y.shape[1]), axis=0)
    sq[...] = total


def last_of(na, nc, u_ref, pieces, spot):
    for s, piece in enumerate(pieces):
        at = rows_of(spot, s, len(pieces), na)
        for c in range(nc):
            yield c, at, u_ref[c, at, :] + piece[pl.ds(c, na, stride=nc), :]


def norm_kernel(na, nc, n, me_ref, u_ref, *refs):
    spot, _ = place(me_ref)
    nb = u_ref.shape[-1]
    total = jnp.zeros((na, nb), F32)
    for _, _, y in last_of(na, nc, u_ref, refs[:n], spot):
        total = total + y * y
    squares = [r[...] for r in refs[n:-1]]
    tiles = [jnp.sum(t, axis=0, keepdims=True) for t in (squares[0], sum(squares[2:], squares[1]), total)]
    refs[-1][...] = jnp.concatenate([*tiles, jnp.zeros((8 - ITERS, nb), F32)], 0)


def finish_kernel(na, nc, me_ref, u_ref, *refs):
    spot, _ = place(me_ref)
    for c, at, y in last_of(na, nc, u_ref, refs[:-1], spot):
        refs[-1][c, at, :] = y


def local(x):
    return pltpu.with_memory_space_constraint(x, pltpu.VMEM)


def call(kernel, outs, scalars, arrays, scratch=(), specs=None, flops=0):
    return pl.pallas_call(
        kernel,
        out_shape=outs,
        in_specs=[SM] * len(scalars) + (specs or [VM] * len(arrays)),
        out_specs=[VM] * len(outs),
        scratch_shapes=list(scratch),
        compiler_params=pltpu.CompilerParams(vmem_limit_bytes=20 << 20),
        cost_estimate=pl.CostEstimate(flops=flops, bytes_accessed=1 << 16, transcendentals=0),
    )(*scalars, *arrays)


def per_device(psi_prev, psi_cur, kin_stretch, kin_radius, potential, angular, pattern, quanta):
    nc, nr, nb = psi_cur.shape
    lam = potential.shape[0]
    nd = lax.axis_size("chan")
    n = nd // TEAM
    na = nr // n
    total_ch = nc * nd
    cb = total_ch // pattern.shape[1]
    me = lax.axis_index("chan").astype(jnp.int32).reshape(1)
    sds = jax.ShapeDtypeStruct

    def swap(x, bits):
        return lax.ppermute(x, "chan", [(i, i ^ bits) for i in range(nd)])

    def across(x, bits):
        return local(swap(x, bits))

    def exchange(pieces):
        return [across(x, hop(i, n) * TEAM) if i else x for i, x in enumerate(pieces)]

    def exchange_all(x):
        lines = [[spot * TEAM + seat for spot in range(n)] for seat in range(TEAM)]
        return local(lax.all_to_all(x, "chan", 0, 0, tiled=True, axis_index_groups=lines))

    def after(x, *others):
        return lax.optimization_barrier((x, *others))[0]

    def gather(x, beside):
        over = local(after(swap(x, 2), *beside))
        return [[y] for y in (x, across(x, 1), over, across(over, 1))]

    def gather_near_far(near, far, near_core, far_core, over):
        rows = [[x, y, z, across(z, 1)] for x, y, z in ((far, far_core, across(far, 2)), (near, near_core, over))]
        return list(zip(*rows))

    piece = pltpu.VMEM((na * nc, nb), F32)
    packed = pltpu.VMEM((n, na * nc, nb), F32)
    square = pltpu.VMEM((8, nb), F32)
    on_chip = pltpu.VMEM((nc, nr, nb), F32)
    natural = sds((nc, nr, nb), F32)
    split = pltpu.VMEM((nd, nc, max(1, na // 2) * nb), BF16)

    def kinetic(prev, cur=(), pieces=(), base=(), n_out=0, out=(), behind=()):
        kernel = functools.partial(kinetic_kernel, na, nc, n, len(pieces), len(base), n_out, len(behind))
        arrays = [kin_stretch, kin_radius, prev, *pieces, *base, *cur]
        outs = [packed] if n_out == 1 else [piece] * n_out
        specs = [VM] * len(arrays) + [ANY] * len(behind)
        return call(kernel, [*outs, on_chip, *out], [me, quanta.T], arrays + list(behind), (), specs)

    def mix(sources, flops=0):
        arrays = [local(coup), local(potential), *(x for source in sources for x in source)]
        kernel = functools.partial(mix_kernel, nc, n, len(sources[0]))
        return call(kernel, [piece] * n, [me], arrays, [split, split], flops=flops)

    def group(pieces, behind=()):
        k = len(pieces)
        specs = [VM] * k + [ANY] * len(behind)
        kernel = functools.partial(group_kernel, k)
        return call(kernel, [pltpu.VMEM((k, na * nc, nb), F32)], [me], [*pieces, *behind], (), specs)[0]

    def group_join(ws, us, behind=()):
        k = len(ws)
        outs = [piece] * k + [pltpu.VMEM((k, na * nc, nb), F32), square]
        specs = [VM] * (2 * k) + [ANY] * len(behind)
        return call(functools.partial(group_join_kernel, k), outs, [me], [*ws, *us, *behind], (), specs)

    (coup,) = call(
        functools.partial(coupling_kernel, cb, nc, n),
        [pltpu.VMEM((lam, 2, n, nc, total_ch), BF16)],
        [me, pattern],
        [pltpu.with_memory_space_constraint(angular, pltpu.HBM)],
        [pltpu.VMEM((lam, n, nc, total_ch), F32), pltpu.SemaphoreType.DMA((lam * n,))],
        [pl.BlockSpec(memory_space=pltpu.HBM)],
        flops=0,
    )
    v1 = exchange(call(functools.partial(to_pieces_kernel, na, nc), [piece] * n, [me], [psi_cur]))
    near, far = near_far(v1)
    near = group(near)
    near_core, near_over = across(near, 1), across(near, 2)
    u1, u1_nat = kinetic(psi_prev, [psi_cur], n_out=1)
    u1 = exchange_all(after(u1, near_over))
    far = group(far, [coup, u1_nat])
    w1 = mix(gather_near_far(near, far, near_core, across(far, 1), near_over), 5000000000)
    w1_c = exchange(w1)
    v2, s2 = call(functools.partial(join_kernel, n), [packed, square], [me], [u1, *w1])
    *u2, _, v2_nat = kinetic(psi_cur, pieces=w1_c, base=[u1_nat], n_out=n, out=[on_chip])
    w2 = near_far(mix(gather(v2, w1_c[1:]), 0))
    u2 = near_far(exchange(u2))
    *v3_near, near, s3 = group_join(w2[0], u2[0])
    *v3_far, far, s3_far = group_join(w2[1], u2[1], [near])
    v3 = exchange([v3_near[0], *v3_far, v3_near[1]])
    u3, prev_out = kinetic(v2_nat, pieces=v3, out=[natural])
    near_over = local(after(swap(near, 2), v3[1]))
    w3 = exchange(mix(gather_near_far(near, far, across(near, 1), across(far, 1), near_over), 0))
    (sums,) = call(functools.partial(norm_kernel, na, nc, n), [sds((8, nb), F32)], [me], [u3, *w3, s2, s3, s3_far])
    (cur_out,) = call(functools.partial(finish_kernel, na, nc), [natural], [me], [u3, *w3])
    sums = (sums + swap(sums, 1)) + (swap(sums, 2) + swap(sums, 3))
    bit = TEAM
    while bit < nd:
        sums = sums + swap(sums, bit)
        bit *= 2
    norms = jnp.sum(sums[:ITERS], axis=1) / (total_ch * nr * nb)
    return prev_out, cur_out, norms


def solution(mesh):
    return jax.shard_map(
        per_device,
        mesh=mesh,
        in_specs=(
            P(("groups", "chan"), None, None),
            P(("groups", "chan"), None, None),
            P(),
            P(),
            P(),
            P("groups", None, None),
            P("groups", None),
            P(("groups", "chan"), None),
        ),
        out_specs=(
            P(("groups", "chan"), None, None),
            P(("groups", "chan"), None, None),
            P("groups"),
        ),
        check_vma=False,
    )
```

```python
import functools

import jax
import jax.numpy as jnp
import numpy as np
from jax import lax
from jax.experimental import pallas as pl
from jax.experimental.pallas import tpu as pltpu
from jax.sharding import PartitionSpec as P

JL_MAX = 40
ITERS = 3
TEAM = 4
F32 = jnp.float32
BF16 = jnp.bfloat16
VM = pl.BlockSpec(memory_space=pltpu.VMEM)
SM = pl.BlockSpec(memory_space=pltpu.SMEM)
ANY = pl.BlockSpec(memory_space=pl.ANY)


def hop(i, n):
    return i % (n - 1) + 1 if i else 0


def place(me_ref):
    return me_ref[0] // TEAM, me_ref[0] % TEAM


def rows_of(spot, s, n, na):
    return pl.ds(pl.multiple_of((spot ^ hop(s, n)) * na, na), na)


def halves(x):
    hi = x.astype(BF16)
    return hi, (x - hi.astype(F32)).astype(BF16)


def product(a, b):
    return sum(jnp.dot(a[i], b[j], preferred_element_type=F32) for i, j in ((0, 1), (1, 0), (0, 0)))


def to_pieces_kernel(na, nc, me_ref, x_ref, *outs):
    spot, _ = place(me_ref)
    for s, out in enumerate(outs):
        for c in range(nc):
            out[pl.ds(c, na, stride=nc), :] = x_ref[c, rows_of(spot, s, len(outs), na), :]


def kinetic_kernel(na, nc, n, n_in, based, n_out, n_behind, me_ref, quanta, ks, kr, prev, *refs):
    spot, _ = place(me_ref)
    refs = list(refs)
    take = lambda k: [refs.pop(0) for _ in range(k)]
    pieces = take(n_in)
    base = refs.pop(0) if based else None
    cur = None if n_in else refs.pop(0)
    take(n_behind)
    u_refs = take(n_out)
    y_ref = refs.pop(0)
    cur = refs.pop(0) if n_in else cur
    nr, nb = prev.shape[1:]

    def placed(some):
        if len(some) == 1:
            return [(some[0].at[z], pl.ds(z * na, na)) for z in range(n)]
        return [(ref, rows_of(spot, s, n, na)) for s, ref in enumerate(some)]

    kstr = halves(2.0 * ks[...])
    krad = halves(2.0 * kr[...])
    stretch = 1.0 + lax.broadcasted_iota(jnp.int32, (nr, nb), 0).astype(F32) / nr
    radius = 1.0 + 3.0 * lax.broadcasted_iota(jnp.int32, (nr, nb), 1).astype(F32) / nb
    rotation = 1.0 / (stretch * stretch)
    orbital = 1.0 / (radius * radius)
    scale = np.float32(0.3 / (JL_MAX * (JL_MAX - 1)))
    group = min(8, nc)
    for start in range(0, nc, group):
        chans = range(start, start + group)
        for piece, at in placed(pieces):
            for c in chans:
                x = piece[pl.ds(c, na, stride=nc), :]
                cur[c, at, :] = x + base[c, at, :] if based else x
        tiles = [cur[c] for c in chans]
        mixed_a = product(kstr, halves(jnp.concatenate(tiles, 1)))
        mixed_b = product(halves(jnp.concatenate(tiles, 0)), krad)
        for i, c in enumerate(chans):
            j = quanta[0, c].astype(F32)
            l = quanta[1, c].astype(F32)
            barrier = orbital * (scale * (l * (l + 1.0))) + rotation * (scale * (j * (j + 1.0))) - 0.2
            y = mixed_a[:, i * nb : (i + 1) * nb] + mixed_b[i * nr : (i + 1) * nr]
            y_ref[c] = y + barrier * tiles[i] - prev[c]
        for u, at in placed(u_refs):
            for c in chans:
                u[pl.ds(c, na, stride=nc), :] = y_ref[c, at, :]


def coupling_kernel(cb, nc, n, me_ref, pat_ref, ang_ref, out_ref, buf, sems):
    spot, seat = place(me_ref)
    lam, _, tot = ang_ref.shape

    def row(s):
        return ((spot ^ hop(s, n)) * TEAM + seat) * nc

    copies = [
        pltpu.make_async_copy(
            ang_ref.at[m, pl.ds(pl.multiple_of(row(z), nc), nc), :], buf.at[m, z], sems.at[m * n + z]
        )
        for m in range(lam)
        for z in range(n)
    ]
    for copy in copies:
        copy.start()
    lane = lax.broadcasted_iota(jnp.int32, (nc, tot), 1) // cb
    for copy in copies:
        copy.wait()
    for z in range(n):
        factor = jnp.zeros((nc, tot), F32)
        for k in range(tot // cb):
            factor = jnp.where(lane == k, pat_ref[row(z) // cb, k].astype(F32), factor)
        for m in range(lam):
            val = buf[m, z] * factor
            hi = val.astype(BF16)
            out_ref[m, 0, z] = hi
            out_ref[m, 1, z] = (val - hi.astype(F32)).astype(BF16)


def mix_kernel(nc, n, n_ref, me_ref, coup, pot, *refs):
    spot, seat = place(me_ref)
    sources, pieces = refs[: TEAM * n_ref], refs[TEAM * n_ref : -2]
    xs_hi, xs_lo = refs[-2:]
    rows, nb = pieces[0].shape
    na, ch = rows // nc, n * nc
    lam, tot = coup.shape[0], coup.shape[-1]
    step = max(1, na // 2)
    for k0 in range(0, na, step):
        ks = range(k0, k0 + step)
        for m in range(TEAM):
            for s in range(n):
                if n_ref == 1:
                    z, src = s, sources[m].at[s]
                else:
                    far = s % (n - 1) > 0
                    z, src = spot ^ hop(s, n), sources[m * 2 + (not far)].at[s - 1 if far else s // (n - 1)]
                x = jnp.concatenate([src[k * nc : (k + 1) * nc] for k in ks], 1)
                hi = x.astype(BF16)
                xs_hi[z * TEAM + (seat ^ m)] = hi
                xs_lo[z * TEAM + (seat ^ m)] = (x - hi.astype(F32)).astype(BF16)
        x_hi = xs_hi[...].reshape(tot, step * nb)
        x_lo = xs_lo[...].reshape(tot, step * nb)
        acc = None
        for m in range(lam):
            both = coup[m].reshape(2 * ch, tot)
            p = jnp.dot(both, x_hi, preferred_element_type=F32)
            p = p[:ch] + p[ch:] + jnp.dot(both[:ch], x_lo, preferred_element_type=F32)
            w = jnp.concatenate([pot[m, pl.ds(spot * na + k, 1), :] for k in ks], 1)
            p = p * (2.0 * w)
            acc = p if acc is None else acc + p
        for s, piece in enumerate(pieces):
            for i, k in enumerate(ks):
                piece[k * nc : (k + 1) * nc] = acc[s * nc : (s + 1) * nc, i * nb : (i + 1) * nb]


def near_far(pieces):
    return [pieces[0], pieces[-1]], pieces[1:-1]


def group_kernel(n, me_ref, *refs):
    for s in range(n):
        refs[-1][s] = refs[s][...]


def join_kernel(n, me_ref, u_ref, *refs):
    spot, _ = place(me_ref)
    out, sq = refs[-2:]
    total = 0.0
    for s in range(n):
        at = spot ^ hop(s, n)
        y = refs[s][...] + u_ref[at]
        out[at] = y
        total = total + jnp.sum((y * y).reshape(-1, 8, y.shape[1]), axis=0)
    sq[...] = total


def group_join_kernel(n, me_ref, *refs):
    ws, us, outs, (out, sq) = refs[:n], refs[n : 2 * n], refs[-2 - n : -2], refs[-2:]
    total = 0.0
    for s in range(n):
        y = ws[s][...] + us[s][...]
        out[s] = y
        outs[s][...] = y
        total = total + jnp.sum((y * y).reshape(-1, 8, y.shape[1]), axis=0)
    sq[...] = total


def last_of(na, nc, u_ref, pieces, spot):
    for s, piece in enumerate(pieces):
        at = rows_of(spot, s, len(pieces), na)
        for c in range(nc):
            yield c, at, u_ref[c, at, :] + piece[pl.ds(c, na, stride=nc), :]


def norm_kernel(na, nc, n, me_ref, u_ref, *refs):
    spot, _ = place(me_ref)
    nb = u_ref.shape[-1]
    total = jnp.zeros((na, nb), F32)
    for _, _, y in last_of(na, nc, u_ref, refs[:n], spot):
        total = total + y * y
    squares = [r[...] for r in refs[n:-1]]
    tiles = [jnp.sum(t, axis=0, keepdims=True) for t in (squares[0], sum(squares[2:], squares[1]), total)]
    refs[-1][...] = jnp.concatenate([*tiles, jnp.zeros((8 - ITERS, nb), F32)], 0)


def finish_kernel(na, nc, me_ref, u_ref, *refs):
    spot, _ = place(me_ref)
    for c, at, y in last_of(na, nc, u_ref, refs[:-1], spot):
        refs[-1][c, at, :] = y


def local(x):
    return pltpu.with_memory_space_constraint(x, pltpu.VMEM)


def call(kernel, outs, scalars, arrays, scratch=(), specs=None, flops=0):
    return pl.pallas_call(
        kernel,
        out_shape=outs,
        in_specs=[SM] * len(scalars) + (specs or [VM] * len(arrays)),
        out_specs=[VM] * len(outs),
        scratch_shapes=list(scratch),
        compiler_params=pltpu.CompilerParams(vmem_limit_bytes=20 << 20),
        cost_estimate=pl.CostEstimate(flops=flops, bytes_accessed=1 << 16, transcendentals=0),
    )(*scalars, *arrays)


def per_device(psi_prev, psi_cur, kin_stretch, kin_radius, potential, angular, pattern, quanta):
    nc, nr, nb = psi_cur.shape
    lam = potential.shape[0]
    nd = lax.axis_size("chan")
    n = nd // TEAM
    na = nr // n
    total_ch = nc * nd
    cb = total_ch // pattern.shape[1]
    me = lax.axis_index("chan").astype(jnp.int32).reshape(1)
    sds = jax.ShapeDtypeStruct

    def swap(x, bits):
        return lax.ppermute(x, "chan", [(i, i ^ bits) for i in range(nd)])

    def across(x, bits):
        return local(swap(x, bits))

    def exchange(pieces):
        return [across(x, hop(i, n) * TEAM) if i else x for i, x in enumerate(pieces)]

    def exchange_all(x):
        lines = [[spot * TEAM + seat for spot in range(n)] for seat in range(TEAM)]
        return local(lax.all_to_all(x, "chan", 0, 0, tiled=True, axis_index_groups=lines))

    def after(x, *others):
        return lax.optimization_barrier((x, *others))[0]

    def gather(x, beside):
        over = local(after(swap(x, 2), *beside))
        return [[y] for y in (x, across(x, 1), over, across(over, 1))]

    def gather_near_far(near, far, near_core, far_core, over):
        rows = [[x, y, z, across(z, 1)] for x, y, z in ((far, far_core, across(far, 2)), (near, near_core, over))]
        return list(zip(*rows))

    piece = pltpu.VMEM((na * nc, nb), F32)
    packed = pltpu.VMEM((n, na * nc, nb), F32)
    square = pltpu.VMEM((8, nb), F32)
    on_chip = pltpu.VMEM((nc, nr, nb), F32)
    natural = sds((nc, nr, nb), F32)
    split = pltpu.VMEM((nd, nc, max(1, na // 2) * nb), BF16)

    def kinetic(prev, cur=(), pieces=(), base=(), n_out=0, out=(), behind=()):
        kernel = functools.partial(kinetic_kernel, na, nc, n, len(pieces), len(base), n_out, len(behind))
        arrays = [kin_stretch, kin_radius, prev, *pieces, *base, *cur]
        outs = [packed] if n_out == 1 else [piece] * n_out
        specs = [VM] * len(arrays) + [ANY] * len(behind)
        return call(kernel, [*outs, on_chip, *out], [me, quanta.T], arrays + list(behind), (), specs)

    def mix(sources, flops=0):
        arrays = [local(coup), local(potential), *(x for source in sources for x in source)]
        kernel = functools.partial(mix_kernel, nc, n, len(sources[0]))
        return call(kernel, [piece] * n, [me], arrays, [split, split], flops=flops)

    def group(pieces, behind=()):
        k = len(pieces)
        specs = [VM] * k + [ANY] * len(behind)
        kernel = functools.partial(group_kernel, k)
        return call(kernel, [pltpu.VMEM((k, na * nc, nb), F32)], [me], [*pieces, *behind], (), specs)[0]

    def group_join(ws, us, behind=()):
        k = len(ws)
        outs = [piece] * k + [pltpu.VMEM((k, na * nc, nb), F32), square]
        specs = [VM] * (2 * k) + [ANY] * len(behind)
        return call(functools.partial(group_join_kernel, k), outs, [me], [*ws, *us, *behind], (), specs)

    (coup,) = call(
        functools.partial(coupling_kernel, cb, nc, n),
        [pltpu.VMEM((lam, 2, n, nc, total_ch), BF16)],
        [me, pattern],
        [pltpu.with_memory_space_constraint(angular, pltpu.HBM)],
        [pltpu.VMEM((lam, n, nc, total_ch), F32), pltpu.SemaphoreType.DMA((lam * n,))],
        [pl.BlockSpec(memory_space=pltpu.HBM)],
        flops=0,
    )
    v1 = exchange(call(functools.partial(to_pieces_kernel, na, nc), [piece] * n, [me], [psi_cur]))
    near, far = near_far(v1)
    near = group(near)
    near_core, near_over = across(near, 1), across(near, 2)
    u1, u1_nat = kinetic(psi_prev, [psi_cur], n_out=1)
    u1 = exchange_all(after(u1, near_over))
    far = group(far, [coup, u1_nat])
    w1 = mix(gather_near_far(near, far, near_core, across(far, 1), near_over), 5000000000)
    w1_c = exchange(w1)
    v2, s2 = call(functools.partial(join_kernel, n), [packed, square], [me], [u1, *w1])
    *u2, _, v2_nat = kinetic(psi_cur, pieces=w1_c, base=[u1_nat], n_out=n, out=[on_chip])
    w2 = near_far(mix(gather(v2, w1_c[1:]), 0))
    u2 = near_far(exchange(u2))
    *v3_near, near, s3 = group_join(w2[0], u2[0])
    *v3_far, far, s3_far = group_join(w2[1], u2[1], [near])
    v3 = exchange([v3_near[0], *v3_far, v3_near[1]])
    u3, prev_out = kinetic(v2_nat, pieces=v3, out=[natural])
    near_over = local(after(swap(near, 2), v3[1]))
    w3 = exchange(mix(gather_near_far(near, far, across(near, 1), across(far, 1), near_over), 0))
    (sums,) = call(functools.partial(norm_kernel, na, nc, n), [sds((8, nb), F32)], [me], [u3, *w3, s2, s3, s3_far])
    (cur_out,) = call(functools.partial(finish_kernel, na, nc), [natural], [me], [u3, *w3])
    bit = 1
    while bit < nd:
        sums = (sums + swap(sums, bit)) + (swap(sums, 2 * bit) + swap(sums, 3 * bit))
        bit *= 4
    norms = jnp.sum(sums[:ITERS], axis=1) / (total_ch * nr * nb)
    return prev_out, cur_out, norms


def solution(mesh):
    return jax.shard_map(
        per_device,
        mesh=mesh,
        in_specs=(
            P(("groups", "chan"), None, None),
            P(("groups", "chan"), None, None),
            P(),
            P(),
            P(),
            P("groups", None, None),
            P("groups", None),
            P(("groups", "chan"), None),
        ),
        out_specs=(
            P(("groups", "chan"), None, None),
            P(("groups", "chan"), None, None),
            P("groups"),
        ),
        check_vma=False,
    )
```

```python
import functools

import jax
import jax.numpy as jnp
import numpy as np
from jax import lax
from jax.experimental import pallas as pl
from jax.experimental.pallas import tpu as pltpu
from jax.sharding import PartitionSpec as P

JL_MAX = 40
ITERS = 3
TEAM = 4
F32 = jnp.float32
BF16 = jnp.bfloat16
VM = pl.BlockSpec(memory_space=pltpu.VMEM)
SM = pl.BlockSpec(memory_space=pltpu.SMEM)
ANY = pl.BlockSpec(memory_space=pl.ANY)


def hop(i, n):
    return i % (n - 1) + 1 if i else 0


def place(me_ref):
    return me_ref[0] // TEAM, me_ref[0] % TEAM


def rows_of(spot, s, n, na):
    return pl.ds(pl.multiple_of((spot ^ hop(s, n)) * na, na), na)


def halves(x):
    hi = x.astype(BF16)
    return hi, (x - hi.astype(F32)).astype(BF16)


def product(a, b):
    return sum(jnp.dot(a[i], b[j], preferred_element_type=F32) for i, j in ((0, 1), (1, 0), (0, 0)))


def to_pieces_kernel(na, nc, me_ref, x_ref, *outs):
    spot, _ = place(me_ref)
    for s, out in enumerate(outs):
        for c in range(nc):
            out[pl.ds(c, na, stride=nc), :] = x_ref[c, rows_of(spot, s, len(outs), na), :]


def kinetic_kernel(na, nc, n, n_in, based, n_out, n_behind, me_ref, quanta, ks, kr, prev, *refs):
    spot, _ = place(me_ref)
    refs = list(refs)
    take = lambda k: [refs.pop(0) for _ in range(k)]
    pieces = take(n_in)
    base = refs.pop(0) if based else None
    cur = None if n_in else refs.pop(0)
    take(n_behind)
    u_refs = take(n_out)
    y_ref = refs.pop(0)
    cur = refs.pop(0) if n_in else cur
    nr, nb = prev.shape[1:]

    def placed(some):
        if len(some) == 1:
            return [(some[0].at[z], pl.ds(z * na, na)) for z in range(n)]
        return [(ref, rows_of(spot, s, n, na)) for s, ref in enumerate(some)]

    kstr = halves(2.0 * ks[...])
    krad = halves(2.0 * kr[...])
    stretch = 1.0 + lax.broadcasted_iota(jnp.int32, (nr, nb), 0).astype(F32) / nr
    radius = 1.0 + 3.0 * lax.broadcasted_iota(jnp.int32, (nr, nb), 1).astype(F32) / nb
    rotation = 1.0 / (stretch * stretch)
    orbital = 1.0 / (radius * radius)
    scale = np.float32(0.3 / (JL_MAX * (JL_MAX - 1)))
    group = min(16, nc)
    for start in range(0, nc, group):
        chans = range(start, start + group)
        for piece, at in placed(pieces):
            for c in chans:
                x = piece[pl.ds(c, na, stride=nc), :]
                cur[c, at, :] = x + base[c, at, :] if based else x
        tiles = [cur[c] for c in chans]
        mixed_a = product(kstr, halves(jnp.concatenate(tiles, 1)))
        mixed_b = product(halves(jnp.concatenate(tiles, 0)), krad)
        for i, c in enumerate(chans):
            j = quanta[0, c].astype(F32)
            l = quanta[1, c].astype(F32)
            barrier = orbital * (scale * (l * (l + 1.0))) + rotation * (scale * (j * (j + 1.0))) - 0.2
            y = mixed_a[:, i * nb : (i + 1) * nb] + mixed_b[i * nr : (i + 1) * nr]
            y_ref[c] = y + barrier * tiles[i] - prev[c]
        for u, at in placed(u_refs):
            for c in chans:
                u[pl.ds(c, na, stride=nc), :] = y_ref[c, at, :]


def coupling_kernel(cb, nc, n, me_ref, pat_ref, ang_ref, out_ref, buf, sems):
    spot, seat = place(me_ref)
    lam, _, tot = ang_ref.shape

    def row(s):
        return ((spot ^ hop(s, n)) * TEAM + seat) * nc

    copies = [
        pltpu.make_async_copy(
            ang_ref.at[m, pl.ds(pl.multiple_of(row(z), nc), nc), :], buf.at[m, z], sems.at[m * n + z]
        )
        for m in range(lam)
        for z in range(n)
    ]
    for copy in copies:
        copy.start()
    lane = lax.broadcasted_iota(jnp.int32, (nc, tot), 1) // cb
    for copy in copies:
        copy.wait()
    for z in range(n):
        factor = jnp.zeros((nc, tot), F32)
        for k in range(tot // cb):
            factor = jnp.where(lane == k, pat_ref[row(z) // cb, k].astype(F32), factor)
        for m in range(lam):
            val = buf[m, z] * factor
            hi = val.astype(BF16)
            out_ref[m, 0, z] = hi
            out_ref[m, 1, z] = (val - hi.astype(F32)).astype(BF16)


def mix_kernel(nc, n, n_ref, me_ref, coup, pot, *refs):
    spot, seat = place(me_ref)
    sources, pieces = refs[: TEAM * n_ref], refs[TEAM * n_ref : -2]
    xs_hi, xs_lo = refs[-2:]
    rows, nb = pieces[0].shape
    na, ch = rows // nc, n * nc
    lam, tot = coup.shape[0], coup.shape[-1]
    step = max(1, na // 2)
    for k0 in range(0, na, step):
        ks = range(k0, k0 + step)
        for m in range(TEAM):
            for s in range(n):
                if n_ref == 1:
                    z, src = s, sources[m].at[s]
                else:
                    far = s % (n - 1) > 0
                    z, src = spot ^ hop(s, n), sources[m * 2 + (not far)].at[s - 1 if far else s // (n - 1)]
                x = jnp.concatenate([src[k * nc : (k + 1) * nc] for k in ks], 1)
                hi = x.astype(BF16)
                xs_hi[z * TEAM + (seat ^ m)] = hi
                xs_lo[z * TEAM + (seat ^ m)] = (x - hi.astype(F32)).astype(BF16)
        x_hi = xs_hi[...].reshape(tot, step * nb)
        x_lo = xs_lo[...].reshape(tot, step * nb)
        acc = None
        for m in range(lam):
            both = coup[m].reshape(2 * ch, tot)
            p = jnp.dot(both, x_hi, preferred_element_type=F32)
            p = p[:ch] + p[ch:] + jnp.dot(both[:ch], x_lo, preferred_element_type=F32)
            w = jnp.concatenate([pot[m, pl.ds(spot * na + k, 1), :] for k in ks], 1)
            p = p * (2.0 * w)
            acc = p if acc is None else acc + p
        for s, piece in enumerate(pieces):
            for i, k in enumerate(ks):
                piece[k * nc : (k + 1) * nc] = acc[s * nc : (s + 1) * nc, i * nb : (i + 1) * nb]


def near_far(pieces):
    return [pieces[0], pieces[-1]], pieces[1:-1]


def group_kernel(n, me_ref, *refs):
    for s in range(n):
        refs[-1][s] = refs[s][...]


def join_kernel(n, me_ref, u_ref, *refs):
    spot, _ = place(me_ref)
    out, sq = refs[-2:]
    total = 0.0
    for s in range(n):
        at = spot ^ hop(s, n)
        y = refs[s][...] + u_ref[at]
        out[at] = y
        total = total + jnp.sum((y * y).reshape(-1, 8, y.shape[1]), axis=0)
    sq[...] = total


def group_join_kernel(n, me_ref, *refs):
    ws, us, outs, (out, sq) = refs[:n], refs[n : 2 * n], refs[-2 - n : -2], refs[-2:]
    total = 0.0
    for s in range(n):
        y = ws[s][...] + us[s][...]
        out[s] = y
        outs[s][...] = y
        total = total + jnp.sum((y * y).reshape(-1, 8, y.shape[1]), axis=0)
    sq[...] = total


def last_of(na, nc, u_ref, pieces, spot):
    for s, piece in enumerate(pieces):
        at = rows_of(spot, s, len(pieces), na)
        for c in range(nc):
            yield c, at, u_ref[c, at, :] + piece[pl.ds(c, na, stride=nc), :]


def norm_kernel(na, nc, n, me_ref, u_ref, *refs):
    spot, _ = place(me_ref)
    nb = u_ref.shape[-1]
    total = jnp.zeros((na, nb), F32)
    for _, _, y in last_of(na, nc, u_ref, refs[:n], spot):
        total = total + y * y
    squares = [r[...] for r in refs[n:-1]]
    tiles = [jnp.sum(t, axis=0, keepdims=True) for t in (squares[0], sum(squares[2:], squares[1]), total)]
    refs[-1][...] = jnp.concatenate([*tiles, jnp.zeros((8 - ITERS, nb), F32)], 0)


def finish_kernel(na, nc, me_ref, u_ref, *refs):
    spot, _ = place(me_ref)
    for c, at, y in last_of(na, nc, u_ref, refs[:-1], spot):
        refs[-1][c, at, :] = y


def local(x):
    return pltpu.with_memory_space_constraint(x, pltpu.VMEM)


def call(kernel, outs, scalars, arrays, scratch=(), specs=None, flops=0):
    return pl.pallas_call(
        kernel,
        out_shape=outs,
        in_specs=[SM] * len(scalars) + (specs or [VM] * len(arrays)),
        out_specs=[VM] * len(outs),
        scratch_shapes=list(scratch),
        compiler_params=pltpu.CompilerParams(vmem_limit_bytes=20 << 20),
        cost_estimate=pl.CostEstimate(flops=flops, bytes_accessed=1 << 16, transcendentals=0),
    )(*scalars, *arrays)


def per_device(psi_prev, psi_cur, kin_stretch, kin_radius, potential, angular, pattern, quanta):
    nc, nr, nb = psi_cur.shape
    lam = potential.shape[0]
    nd = lax.axis_size("chan")
    n = nd // TEAM
    na = nr // n
    total_ch = nc * nd
    cb = total_ch // pattern.shape[1]
    me = lax.axis_index("chan").astype(jnp.int32).reshape(1)
    sds = jax.ShapeDtypeStruct

    def swap(x, bits):
        return lax.ppermute(x, "chan", [(i, i ^ bits) for i in range(nd)])

    def across(x, bits):
        return local(swap(x, bits))

    def exchange(pieces):
        return [across(x, hop(i, n) * TEAM) if i else x for i, x in enumerate(pieces)]

    def exchange_all(x):
        lines = [[spot * TEAM + seat for spot in range(n)] for seat in range(TEAM)]
        return local(lax.all_to_all(x, "chan", 0, 0, tiled=True, axis_index_groups=lines))

    def after(x, *others):
        return lax.optimization_barrier((x, *others))[0]

    def gather(x, beside):
        over = local(after(swap(x, 2), *beside))
        return [[y] for y in (x, across(x, 1), over, across(over, 1))]

    def gather_near_far(near, far, near_core, far_core, over):
        rows = [[x, y, z, across(z, 1)] for x, y, z in ((far, far_core, across(far, 2)), (near, near_core, over))]
        return list(zip(*rows))

    piece = pltpu.VMEM((na * nc, nb), F32)
    packed = pltpu.VMEM((n, na * nc, nb), F32)
    square = pltpu.VMEM((8, nb), F32)
    on_chip = pltpu.VMEM((nc, nr, nb), F32)
    natural = sds((nc, nr, nb), F32)
    split = pltpu.VMEM((nd, nc, max(1, na // 2) * nb), BF16)

    def kinetic(prev, cur=(), pieces=(), base=(), n_out=0, out=(), behind=()):
        kernel = functools.partial(kinetic_kernel, na, nc, n, len(pieces), len(base), n_out, len(behind))
        arrays = [kin_stretch, kin_radius, prev, *pieces, *base, *cur]
        outs = [packed] if n_out == 1 else [piece] * n_out
        specs = [VM] * len(arrays) + [ANY] * len(behind)
        return call(kernel, [*outs, on_chip, *out], [me, quanta.T], arrays + list(behind), (), specs)

    def mix(sources, flops=0):
        arrays = [local(coup), local(potential), *(x for source in sources for x in source)]
        kernel = functools.partial(mix_kernel, nc, n, len(sources[0]))
        return call(kernel, [piece] * n, [me], arrays, [split, split], flops=flops)

    def group(pieces, behind=()):
        k = len(pieces)
        specs = [VM] * k + [ANY] * len(behind)
        kernel = functools.partial(group_kernel, k)
        return call(kernel, [pltpu.VMEM((k, na * nc, nb), F32)], [me], [*pieces, *behind], (), specs)[0]

    def group_join(ws, us, behind=()):
        k = len(ws)
        outs = [piece] * k + [pltpu.VMEM((k, na * nc, nb), F32), square]
        specs = [VM] * (2 * k) + [ANY] * len(behind)
        return call(functools.partial(group_join_kernel, k), outs, [me], [*ws, *us, *behind], (), specs)

    (coup,) = call(
        functools.partial(coupling_kernel, cb, nc, n),
        [pltpu.VMEM((lam, 2, n, nc, total_ch), BF16)],
        [me, pattern],
        [pltpu.with_memory_space_constraint(angular, pltpu.HBM)],
        [pltpu.VMEM((lam, n, nc, total_ch), F32), pltpu.SemaphoreType.DMA((lam * n,))],
        [pl.BlockSpec(memory_space=pltpu.HBM)],
        flops=0,
    )
    v1 = exchange(call(functools.partial(to_pieces_kernel, na, nc), [piece] * n, [me], [psi_cur]))
    near, far = near_far(v1)
    near = group(near)
    near_core, near_over = across(near, 1), across(near, 2)
    u1, u1_nat = kinetic(psi_prev, [psi_cur], n_out=1)
    u1 = exchange_all(after(u1, near_over))
    far = group(far, [coup, u1_nat])
    w1 = mix(gather_near_far(near, far, near_core, across(far, 1), near_over), 5000000000)
    w1_c = exchange(w1)
    v2, s2 = call(functools.partial(join_kernel, n), [packed, square], [me], [u1, *w1])
    *u2, _, v2_nat = kinetic(psi_cur, pieces=w1_c, base=[u1_nat], n_out=n, out=[on_chip])
    w2 = near_far(mix(gather(v2, w1_c[1:]), 0))
    u2 = near_far(exchange(u2))
    *v3_near, near, s3 = group_join(w2[0], u2[0])
    *v3_far, far, s3_far = group_join(w2[1], u2[1], [near])
    v3 = exchange([v3_near[0], *v3_far, v3_near[1]])
    u3, prev_out = kinetic(v2_nat, pieces=v3, out=[natural])
    near_over = local(after(swap(near, 2), v3[1]))
    w3 = exchange(mix(gather_near_far(near, far, across(near, 1), across(far, 1), near_over), 0))
    (sums,) = call(functools.partial(norm_kernel, na, nc, n), [sds((8, nb), F32)], [me], [u3, *w3, s2, s3, s3_far])
    (cur_out,) = call(functools.partial(finish_kernel, na, nc), [natural], [me], [u3, *w3])
    bit = 1
    while bit < nd:
        sums = (sums + swap(sums, bit)) + (swap(sums, 2 * bit) + swap(sums, 3 * bit))
        bit *= 4
    norms = jnp.sum(sums[:ITERS], axis=1) / (total_ch * nr * nb)
    return prev_out, cur_out, norms


def solution(mesh):
    return jax.shard_map(
        per_device,
        mesh=mesh,
        in_specs=(
            P(("groups", "chan"), None, None),
            P(("groups", "chan"), None, None),
            P(),
            P(),
            P(),
            P("groups", None, None),
            P("groups", None),
            P(("groups", "chan"), None),
        ),
        out_specs=(
            P(("groups", "chan"), None, None),
            P(("groups", "chan"), None, None),
            P("groups"),
        ),
        check_vma=False,
    )
```
